32 devices in a mesh: ctx: 8 (over z, core), head: 4 (over y, x).
Axes of the slice: x: 2, y: 2, z: 4, core: 2. Of those that a mesh axis runs over, the one named last changes fastest.
Arguments:
- q_latent: bfloat16 [1024, 1536], P('ctx', 'head'), may hold values from -72 to 72
- latent_cache: bfloat16 [1024, 576], P('ctx'), may hold values from -6 to 6
- w_q_up: bfloat16 [1536, 3072], P(None, 'head'), may hold values from -0.15625 to 0.15625
- w_kv_up: bfloat16 [512, 4096], P(None, 'head'), may hold values from -0.25 to 0.25
- w_out: bfloat16 [2048, 7168], P('head', 'ctx'), may hold values from -1 to 1
- token_pos: int32 [1024], P('ctx'), may hold values from 0 to 1023, as said below
- start_offset: int32 [1], replicated, may hold values from 0 to 65535
Outputs:
- layer_out: bfloat16 [1024, 7168], P('ctx', 'head')
The draws below stay inside these ranges and needn't reach their ends.
Inputs may be any that keep to these rules, and one draw needn't show every extreme that they name: `token_pos`: a permutation of 0 to 1023; the 128 tokens of each index of ctx hold consecutive positions in increasing order.
All inputs are finite; a program needn't handle non-finite values.
Results may differ from the reference program's by a relative error of at most 0.035.
Values may be sent and summed in bfloat16 or wider, within the bound.
A program may use at most 64 MiB of HBM per device.

```python
import jax
import jax.numpy as jnp
from jax import lax

D = 7168
QL = 1536
KVL = 512
NOPE = 128
ROPE = 64
VDIM = 128
HEAD_DEV = 4
TOK_DEV = 128
HEADS = 16
TOKENS = 1024
N_HEAD = 4


def draw_q_latent(key, part):
    first = jax.random.fold_in(key, 0)
    values = jax.random.truncated_normal(first, -6.0, 6.0, (TOKENS, QL), jnp.float32)
    return values.astype(jnp.bfloat16)


def draw_token_pos(key, part):
    blocks = TOKENS // TOK_DEV
    order = jax.random.permutation(key, blocks).astype(jnp.int32)
    inside = jnp.arange(TOK_DEV, dtype=jnp.int32)
    return (order[:, None] * TOK_DEV + inside[None, :]).reshape(TOKENS)


def steps_of(stream_key, shape, pieces, least, top_value):
    factor_of = 1.0
    for position, blocks in pieces:
        steps = jax.random.uniform(jax.random.fold_in(jax.random.fold_in(stream_key, 6), position), (blocks,), jnp.float32, least / len(pieces), top_value / len(pieces))
        factor_of = factor_of * jnp.repeat(jnp.exp(steps), shape[position] // blocks).reshape((-1,) + (1,) * (len(shape) - 1 - position))
    return factor_of


def bell_draw(rng, dims, deviation, bound, cuts=(), kind=jnp.bfloat16):
    array = jax.random.normal(rng, dims, jnp.float32) * deviation
    if len(cuts) > 0:
        array = steps_of(rng, dims, cuts, -0.22, 0.18) * array
    return jnp.clip(array, min=-bound, max=bound).astype(kind)


def setup_inputs(seed: int = 0) -> dict:
    key_of = jax.random.split(jax.random.key(seed), 8)
    q_latent = draw_q_latent(jax.random.fold_in(key_of[7], 71), 0)
    latent_cache = bell_draw(key_of[1], (TOKENS, KVL + ROPE), 1.0, 6.0, ((0, 8),))
    w_q_up = bell_draw(key_of[2], (QL, HEADS * (NOPE + ROPE)), QL ** -0.5, 0.15625, ((1, 4),))
    w_kv_up = bell_draw(key_of[3], (KVL, HEADS * (NOPE + VDIM)), KVL ** -0.5, 0.25, ((1, 4),))
    w_out = bell_draw(key_of[4], (HEADS * VDIM, D), (HEADS * VDIM // 64) ** -0.5, 1.0, ((0, 4), (1, 8)))
    token_pos = draw_token_pos(jax.random.fold_in(key_of[7], 71), 0)
    start_offset = jax.random.randint(key_of[6], (1,), 0, 65536).astype(jnp.int32)
    return {"q_latent": q_latent, "latent_cache": latent_cache, "w_q_up": w_q_up, "w_kv_up": w_kv_up, "w_out": w_out, "token_pos": token_pos, "start_offset": start_offset}


negative_fill = -1e30
softmax_scale = 0.135
rope_base = 10000.0


def rotate(values, angle):
    half = ROPE // 2
    cosine = jnp.cos(angle)
    sine = jnp.sin(angle)
    first = values[..., :half]
    second = values[..., half:]
    return jnp.concatenate([first * cosine - second * sine, first * sine + second * cosine], axis=-1)


def reference(q_latent, latent_cache, w_q_up, w_kv_up, w_out, token_pos, start_offset):
    head_count = HEAD_DEV * N_HEAD
    query = jnp.dot(q_latent, w_q_up, preferred_element_type=jnp.float32).reshape(TOKENS, head_count, NOPE + ROPE)
    absolute = (token_pos + start_offset[0]).astype(jnp.float32)
    freqs = rope_base ** (-jnp.arange(ROPE // 2, dtype=jnp.float32) * 2.0 / ROPE)
    angle = absolute[:, None, None] * freqs[None, None, :]
    query_nope = query[..., :NOPE].astype(jnp.bfloat16)
    query_rope = rotate(query[..., NOPE:], angle).astype(jnp.bfloat16)
    latent = latent_cache[:, :KVL]
    key_rope = latent_cache[:, KVL:]
    visible = token_pos[None, :] <= token_pos[:, None]

    def one_head(index):
        columns = lax.dynamic_slice_in_dim(w_kv_up, (index * (NOPE + VDIM)).astype(jnp.int32), NOPE + VDIM, 1)
        expanded = jnp.dot(latent, columns, preferred_element_type=jnp.float32).astype(jnp.bfloat16)
        head_nope = lax.dynamic_index_in_dim(query_nope, index, 1, keepdims=False)
        head_rope = lax.dynamic_index_in_dim(query_rope, index, 1, keepdims=False)
        scores = jnp.dot(head_nope, expanded[:, :NOPE].T, preferred_element_type=jnp.float32)
        scores = scores + jnp.dot(head_rope, key_rope.T, preferred_element_type=jnp.float32)
        scores = jnp.where(visible, scores * softmax_scale, negative_fill)
        largest = jnp.max(scores, axis=-1, keepdims=True)
        weights = jnp.where(visible, jnp.exp(scores - largest), 0.0)
        totals = jnp.sum(weights, axis=-1, keepdims=True)
        summed = jnp.dot(weights.astype(jnp.bfloat16), expanded[:, NOPE:], preferred_element_type=jnp.float32)
        return (summed / totals).astype(jnp.bfloat16)

    per_head = lax.map(one_head, jnp.arange(head_count, dtype=jnp.int32))
    attention = jnp.transpose(per_head, (1, 0, 2)).reshape(TOKENS, head_count * VDIM)
    group_width = HEAD_DEV * VDIM

    def one_group(index):
        start = (index * group_width).astype(jnp.int32)
        columns = lax.dynamic_slice_in_dim(attention, start, group_width, 1)
        rows = lax.dynamic_slice_in_dim(w_out, start, group_width, 0)
        return jnp.dot(columns, rows, preferred_element_type=jnp.float32).astype(jnp.bfloat16)

    def add_group(total, index):
        return total + one_group(index).astype(jnp.float32), None

    total, unused = lax.scan(add_group, jnp.zeros((TOKENS, D), jnp.float32), jnp.arange(N_HEAD, dtype=jnp.int32))
    return total.astype(jnp.bfloat16)
```

```python
import functools

import jax
import jax.numpy as jnp
import numpy as np
from jax import lax
from jax.experimental import pallas as pl
from jax.experimental.pallas import tpu as pltpu
from jax.sharding import PartitionSpec as P

KVL = 512
NOPE = 128
ROPE = 64
VDIM = 128
LANES = KVL + ROPE

negative_fill = -1e30
softmax_scale = 0.135
rope_base = 10000.0
F32 = jnp.float32
BF16 = jnp.bfloat16
MESH = pl.DeviceIdType.MESH


def dot_t(a, b):
    return lax.dot_general(a, b, (((1,), (1,)), ((), ())), preferred_element_type=F32)


def kernel(
    n_c, n_h, heads, rows,
    qlat, lat, wq, wkv, wout, tok_h, freq_h, offset_h,
    out,
    tok, freq, offset, wq_v, wkv_v, w2, qbuf, latbuf, posbuf, qa, score, prob, attbuf,
    pa, ra, ta, qa2, pb, rb, tb, qb2, rbuf, zbuf,
    lsem, qs, qr, lzs, lps, latr, xzs, xzr, xps, xpr, pzs, pzr, pps, ppr, ws, wr, ats, atr,
    sa1, va1, sa2, va2, sb1, vb1, sb2, vb2, zs, zr, os_, or_,
):
    n_z = n_c // 2
    piece = rows // n_h
    n_lo = n_h // 2
    width = w2.shape[2]
    q_block = qbuf.shape[2]
    c = lax.axis_index("ctx")
    h = lax.axis_index("head")
    k = lax.rem(c, 2)
    z = lax.div(c, 2)
    partner = c + 1 - 2 * k
    z_of = [lax.rem(z + d, n_z) for d in range(n_z)]
    h_of = [lax.rem(h + e, n_h) for e in range(n_h)]
    hi, lo = lax.div(h, n_lo), lax.rem(h, n_lo)
    lo_of = [lax.rem(lo + e, n_lo) for e in range(n_lo)]
    c_of = [2 * zz + k for zz in z_of]

    def remote(src, dst, ssem, rsem, cc, hh):
        return pltpu.make_async_remote_copy(
            src_ref=src, dst_ref=dst, send_sem=ssem, recv_sem=rsem,
            device_id=(cc, hh), device_id_type=MESH,
        )

    def slot(cc):
        return latbuf.at[cc]

    barrier = pltpu.get_barrier_semaphore()
    for d in range(1, n_z):
        pl.semaphore_signal(barrier, inc=1, device_id=(c_of[d], h), device_id_type=MESH)
    for e in range(1, n_h):
        pl.semaphore_signal(barrier, inc=1, device_id=(c, h_of[e]), device_id_type=MESH)
    pl.semaphore_signal(barrier, inc=1, device_id=(partner, h), device_id_type=MESH)

    local = [
        pltpu.make_async_copy(qlat, qbuf.at[h], lsem.at[0]),
        pltpu.make_async_copy(wq, wq_v, lsem.at[1]),
        pltpu.make_async_copy(wkv, wkv_v, lsem.at[2]),
        pltpu.make_async_copy(lat, slot(c), lsem.at[3]),
        pltpu.make_async_copy(wout, w2.at[k], lsem.at[4]),
        pltpu.make_async_copy(tok_h, tok, lsem.at[5]),
        pltpu.make_async_copy(freq_h, freq, lsem.at[6]),
        pltpu.make_async_copy(offset_h, offset, lsem.at[7]),
    ]
    for copy in local:
        copy.start()
    pl.semaphore_wait(barrier, n_z + n_h - 1)

    third_rows = LANES // 3
    odd = lax.rem(lo, 2)
    pair = hi * n_lo + lo + 1 - 2 * odd
    mine = pl.ds(pl.multiple_of(odd * third_rows, third_rows), third_rows)
    other = pl.ds(pl.multiple_of((1 - odd) * third_rows, third_rows), third_rows)
    both = pl.ds(2 * third_rows, third_rows)
    sends = []

    def send(*args):
        copy = remote(*args)
        copy.start()
        sends.append(copy)

    for e in range(1, n_h):
        send(qlat, qbuf.at[h], qs.at[e], qr.at[h], c, h_of[e])
    for d in range(n_z - 1, 0, -1):
        send(lat.at[mine, :], latbuf.at[c, mine, :], xzs.at[d], xzr.at[z], c_of[d], h)
    for d in range(n_z - 1, 0, -1):
        send(lat.at[both, :], latbuf.at[c, both, :], lzs.at[d], latr.at[c], c_of[d], h)
    send(lat, slot(c), lps.at[0], latr.at[c], partner, h)
    for d in range(1, n_z):
        send(tok_h, posbuf.at[k, z], pzs.at[d], pzr.at[z], c_of[d], h)
    for copy in local[5:]:
        copy.wait()
    posbuf[k, z] = tok[...]

    for d in range(1, n_z):
        cc = c_of[d]
        remote(lat.at[mine, :], latbuf.at[cc, mine, :], xzs.at[d], xzr.at[z_of[d]], cc, h).wait_recv()
        send(latbuf.at[cc, mine, :], latbuf.at[cc, mine, :], xps.at[d], xpr.at[z_of[d]], c, pair)

    positions = jnp.transpose(jnp.broadcast_to(tok[...].astype(F32), (8, rows)))[:, 0:1]
    absolute = jnp.transpose(jnp.broadcast_to((tok[...] + offset[...]).astype(F32), (8, rows)))[:, 0:1]
    angle = absolute * freq[...]
    cosine, sine = jnp.cos(angle), jnp.sin(angle)
    cos = jnp.concatenate([cosine, cosine], axis=1)
    sin = jnp.concatenate([-sine, sine], axis=1)

    local[0].wait()
    local[1].wait()
    for e in range(1, n_h):
        remote(qlat, qbuf.at[h_of[e]], qs.at[e], qr.at[h_of[e]], c, h_of[e]).wait_recv()
    query = None
    for g in range(n_h):
        term = jnp.dot(qbuf[g], wq_v[g * q_block:(g + 1) * q_block, :], preferred_element_type=F32)
        query = term if query is None else query + term
    local[2].wait()
    for j in range(heads):
        base = j * (NOPE + ROPE)
        nope = query[:, base:base + NOPE].astype(BF16)
        main = dot_t(nope, wkv_v[:, j * 256:j * 256 + NOPE])
        lines = slice(j * rows, (j + 1) * rows)
        qa[lines, 0:KVL] = main.astype(BF16)
        rope = query[:, base + NOPE:base + NOPE + ROPE]
        half = ROPE // 2
        swapped = jnp.concatenate([rope[:, half:], rope[:, :half]], axis=1)
        rotated = rope * cos + swapped * sin
        qa[lines, KVL:LANES] = rotated.astype(BF16)

    for d in range(1, n_z):
        cc = c_of[d]
        remote(lat.at[both, :], latbuf.at[cc, both, :], lzs.at[d], latr.at[cc], cc, h).wait_recv()
        remote(
            latbuf.at[cc, other, :], latbuf.at[cc, other, :], xps.at[d], xpr.at[z_of[d]], c, pair
        ).wait_recv()
        send(slot(c_of[d]), slot(c_of[d]), lps.at[d], latr.at[c_of[d]], partner, h)
    for d in range(1, n_z):
        remote(tok, posbuf.at[k, z_of[d]], pzs.at[d], pzr.at[z_of[d]], c_of[d], h).wait_recv()
    send(posbuf.at[k], posbuf.at[k], pps, ppr, partner, h)
    send(wout, w2.at[k], ws, wr, partner, h)
    local[3].wait()
    for d in range(n_z):
        cc = 2 * z_of[d] + 1 - k
        remote(lat, slot(cc), lps.at[d], latr.at[cc], partner, h).wait_recv()

    remote(posbuf.at[1 - k], posbuf.at[1 - k], pps, ppr, partner, h).wait_recv()
    key_pos = jnp.concatenate([posbuf[cc % 2, cc // 2] for cc in range(n_c)], axis=1).astype(F32)
    latents = jnp.concatenate([latbuf[cc] for cc in range(n_c)], axis=1)
    score[...] = jnp.dot(qa[...], latents, preferred_element_type=F32)
    visible = key_pos <= positions
    sums = []
    for j in range(heads):
        lines = slice(j * rows, (j + 1) * rows)
        s = jnp.where(visible, score[lines, :] * softmax_scale, negative_fill)
        largest = jnp.max(s, axis=-1, keepdims=True)
        weights = jnp.where(visible, jnp.exp(s - largest), 0.0)
        sums.append(jnp.sum(weights, axis=-1, keepdims=True))
        prob[lines, :] = weights.astype(BF16)
    summed = dot_t(prob[...], latents[0:KVL, :])
    for j in range(heads):
        normed = (summed[j * rows:(j + 1) * rows, :] / sums[j]).astype(BF16)
        value = jnp.dot(normed, wkv_v[:, j * 256 + NOPE:(j + 1) * 256], preferred_element_type=F32)
        attbuf[z, :, j * VDIM:(j + 1) * VDIM] = value.astype(BF16)

    for d in range(n_z - 1, 0, -1):
        send(attbuf.at[z], attbuf.at[z], ats.at[d], atr.at[z], c_of[d], h)

    local[4].wait()
    remote(wout, w2.at[1 - k], ws, wr, partner, h).wait_recv()

    def project(d):
        zz = z_of[d]
        if d > 0:
            remote(attbuf.at[zz], attbuf.at[zz], ats.at[d], atr.at[zz], c_of[d], h).wait_recv()
        part = jnp.dot(attbuf[zz], w2[0], preferred_element_type=F32).astype(BF16)
        for i in range(n_h):
            pa[d, i % n_lo, i // n_lo] = part[i * piece:(i + 1) * piece, :]
        for e in range(1, n_lo):
            send(pa.at[d, lo_of[e]], ra.at[d, lo], sa1.at[d, e], va1.at[d, lo], c, hi * n_lo + lo_of[e])
        part = jnp.dot(attbuf[zz], w2[1], preferred_element_type=F32).astype(BF16)
        for i in range(n_h):
            pb[d, i // n_lo, i % n_lo] = part[i * piece:(i + 1) * piece, :]
        send(pb.at[d, 1 - hi], rb.at[d], sb1.at[d], vb1.at[d], c, (1 - hi) * n_lo + lo)

    def second(d):
        total = pa[d, lo].astype(F32)
        for e in range(1, n_lo):
            ll = lo_of[e]
            remote(pa.at[d, ll], ra.at[d, ll], sa1.at[d, e], va1.at[d, ll], c, hi * n_lo + ll).wait_recv()
            total = total + ra[d, ll].astype(F32)
        ta[d] = total.astype(BF16)
        send(ta.at[d, 1 - hi], qa2.at[d], sa2.at[d], va2.at[d], c, (1 - hi) * n_lo + lo)
        remote(pb.at[d, hi], rb.at[d], sb1.at[d], vb1.at[d], c, (1 - hi) * n_lo + lo).wait_recv()
        tb[d] = (pb[d, hi].astype(F32) + rb[d].astype(F32)).astype(BF16)
        for e in range(1, n_lo):
            send(tb.at[d, lo_of[e]], qb2.at[d, lo], sb2.at[d, e], vb2.at[d, lo], c, hi * n_lo + lo_of[e])

    def third(d):
        remote(ta.at[d, hi], qa2.at[d], sa2.at[d], va2.at[d], c, (1 - hi) * n_lo + lo).wait_recv()
        first = (ta[d, hi].astype(F32) + qa2[d].astype(F32)).astype(BF16)
        total = tb[d, lo].astype(F32)
        for e in range(1, n_lo):
            ll = lo_of[e]
            remote(tb.at[d, ll], qb2.at[d, ll], sb2.at[d, e], vb2.at[d, ll], c, hi * n_lo + ll).wait_recv()
            total = total + qb2[d, ll].astype(F32)
        if d == 0:
            zbuf[z, :, 0:width] = first
            zbuf[z, :, width:] = total.astype(BF16)
        else:
            rbuf[d, :, 0:width] = first
            rbuf[d, :, width:] = total.astype(BF16)
            send(rbuf.at[d], zbuf.at[z], zs.at[d], zr.at[z], c_of[d], h)

    def deliver(d):
        zz = z_of[(n_z - d) % n_z]
        if d > 0:
            remote(rbuf.at[0], zbuf.at[zz], zs.at[0], zr.at[zz], partner, h).wait_recv()

        @pl.when(zz != h)
        def _():
            remote(zbuf.at[zz], out.at[h], os_.at[d], or_.at[h], c, zz).start()

        @pl.when(zz == h)
        def _():
            out[h] = zbuf[zz]

    def delivered(d):
        zz = z_of[(n_z - d) % n_z]

        @pl.when(zz != h)
        def _():
            remote(zbuf.at[zz], out.at[h], os_.at[d], or_.at[h], c, zz).wait_send()

    for d in range(n_z + 3):
        if d < n_z:
            project(d)
        if 1 <= d <= n_z:
            second(d - 1)
        if 2 <= d <= n_z + 1:
            third(d - 2)
        if d >= 3:
            deliver(d - 3)
    for e in range(1, n_h):
        hh = h_of[e]
        remote(zbuf.at[0], out.at[hh], os_.at[0], or_.at[hh], c, hh).wait_recv()
    for d in range(n_z):
        delivered(d)
    for copy in sends:
        copy.wait_send()


def shards(n_c, n_h, q_latent, latent_cache, w_q_up, w_kv_up, w_out, token_pos, start_offset):
    rows, q_block = q_latent.shape
    heads = w_q_up.shape[1] // (NOPE + ROPE)
    n_z, n_lo = n_c // 2, n_h // 2
    assert n_z == n_h
    keys = n_c * rows
    width = w_out.shape[1]
    piece = rows // n_h
    freqs = rope_base ** (-np.arange(ROPE // 2) * 2.0 / ROPE)
    dma = pltpu.SemaphoreType.DMA
    anywhere = pl.BlockSpec(memory_space=pltpu.HBM)
    vmem = pl.BlockSpec(memory_space=pltpu.VMEM)
    result = pl.pallas_call(
        functools.partial(kernel, n_c, n_h, heads, rows),
        out_shape=pltpu.VMEM((n_h, piece, 2 * width), BF16),
        in_specs=[anywhere] * 8,
        out_specs=vmem,
        scratch_shapes=[
            pltpu.VMEM((1, rows), jnp.int32),
            pltpu.VMEM((1, ROPE // 2), F32),
            pltpu.VMEM((1, 1), jnp.int32),
            pltpu.VMEM(w_q_up.shape, BF16),
            pltpu.VMEM(w_kv_up.shape, BF16),
            pltpu.VMEM((2,) + w_out.shape, BF16),
            pltpu.VMEM((n_h, rows, q_block), BF16),
            pltpu.VMEM((n_c, LANES, rows), BF16),
            pltpu.VMEM((2, n_z, 1, rows), jnp.int32),
            pltpu.VMEM((heads * rows, LANES), BF16),
            pltpu.VMEM((heads * rows, keys), F32),
            pltpu.VMEM((heads * rows, keys), BF16),
            pltpu.VMEM((n_z, rows, heads * VDIM), BF16),
            pltpu.VMEM((n_z, n_lo, 2, piece, width), BF16),
            pltpu.VMEM((n_z, n_lo, 2, piece, width), BF16),
            pltpu.VMEM((n_z, 2, piece, width), BF16),
            pltpu.VMEM((n_z, piece, width), BF16),
            pltpu.VMEM((n_z, 2, n_lo, piece, width), BF16),
            pltpu.VMEM((n_z, n_lo, piece, width), BF16),
            pltpu.VMEM((n_z, n_lo, piece, width), BF16),
            pltpu.VMEM((n_z, n_lo, piece, width), BF16),
            pltpu.VMEM((n_z, piece, 2 * width), BF16),
            pltpu.VMEM((n_z, piece, 2 * width), BF16),
            dma((8,)),
            dma((n_h,)), dma((n_h,)),
            dma((n_z,)), dma((n_z,)), dma((n_c,)),
            dma((n_z,)), dma((n_z,)), dma((n_z,)), dma((n_z,)),
            dma((n_z,)), dma((n_z,)), dma, dma,
            dma, dma,
            dma((n_z,)), dma((n_z,)),
            dma((n_z, n_lo)), dma((n_z, n_lo)), dma((n_z,)), dma((n_z,)),
            dma((n_z,)), dma((n_z,)), dma((n_z, n_lo)), dma((n_z, n_lo)),
            dma((n_z,)), dma((n_z,)),
            dma((n_z,)), dma((n_h,)),
        ],
        compiler_params=pltpu.CompilerParams(
            collective_id=0, has_side_effects=True, vmem_limit_bytes=67043328 - (768 << 10)
        ),
        name="mla",
    )(q_latent, latent_cache.T, w_q_up, w_kv_up, w_out, token_pos[None, :], freqs.astype(np.float32)[None, :], start_offset[None, :])
    return result.reshape(rows, 2 * width)


def solution(mesh):
    in_specs = (
        P("ctx", "head"),
        P("ctx", None),
        P(None, "head"),
        P(None, "head"),
        P("head", "ctx"),
        P("ctx"),
        P(),
    )
    out_specs = P("ctx", "head")
    body = functools.partial(shards, mesh.shape["ctx"], mesh.shape["head"])
    return jax.shard_map(body, mesh=mesh, in_specs=in_specs, out_specs=out_specs, check_vma=False)
```

```python
import functools

import jax
import jax.numpy as jnp
import numpy as np
from jax import lax
from jax.experimental import pallas as pl
from jax.experimental.pallas import tpu as pltpu
from jax.sharding import PartitionSpec as P

KVL = 512
NOPE = 128
ROPE = 64
VDIM = 128
LANES = KVL + ROPE

negative_fill = -1e30
softmax_scale = 0.135
rope_base = 10000.0
F32 = jnp.float32
BF16 = jnp.bfloat16
MESH = pl.DeviceIdType.MESH


def dot_t(a, b):
    return lax.dot_general(a, b, (((1,), (1,)), ((), ())), preferred_element_type=F32)


def kernel(
    n_c, n_h, heads, rows,
    qlat, lat, wq, wkv, wout, tok_h, freq_h, offset_h,
    out,
    tok, freq, offset, wq_v, wkv_v, w2, qbuf, latbuf, posbuf, qa, score, prob, attbuf,
    pa, ra, ta, qa2, pb, rb, tb, qb2, rbuf,
    lsem, qs, qr, lzs, lps, latr, xzs, xzr, xps, xpr, pzs, pzr, pps, ppr, ws, wr, ats, atr,
    sa1, va1, sa2, va2, sb1, vb1, sb2, vb2, os_, or_,
):
    n_z = n_c // 2
    piece = rows // n_h
    n_lo = n_h // 2
    width = w2.shape[2]
    q_block = qbuf.shape[2]
    c = lax.axis_index("ctx")
    h = lax.axis_index("head")
    k = lax.rem(c, 2)
    z = lax.div(c, 2)
    partner = c + 1 - 2 * k
    z_of = [lax.rem(z + d, n_z) for d in range(n_z)]
    h_of = [lax.rem(h + e, n_h) for e in range(n_h)]
    hi, lo = lax.div(h, n_lo), lax.rem(h, n_lo)
    lo_of = [lax.rem(lo + e, n_lo) for e in range(n_lo)]
    c_of = [2 * zz + k for zz in z_of]

    def remote(src, dst, ssem, rsem, cc, hh):
        return pltpu.make_async_remote_copy(
            src_ref=src, dst_ref=dst, send_sem=ssem, recv_sem=rsem,
            device_id=(cc, hh), device_id_type=MESH,
        )

    def slot(cc):
        return latbuf.at[cc]

    barrier = pltpu.get_barrier_semaphore()
    for d in range(1, n_z):
        pl.semaphore_signal(barrier, inc=1, device_id=(c_of[d], h), device_id_type=MESH)
    for e in range(1, n_h):
        pl.semaphore_signal(barrier, inc=1, device_id=(c, h_of[e]), device_id_type=MESH)
    pl.semaphore_signal(barrier, inc=1, device_id=(partner, h), device_id_type=MESH)

    local = [
        pltpu.make_async_copy(qlat, qbuf.at[h], lsem.at[0]),
        pltpu.make_async_copy(wq, wq_v, lsem.at[1]),
        pltpu.make_async_copy(wkv, wkv_v, lsem.at[2]),
        pltpu.make_async_copy(lat, slot(c), lsem.at[3]),
        pltpu.make_async_copy(wout, w2.at[k], lsem.at[4]),
        pltpu.make_async_copy(tok_h, tok, lsem.at[5]),
        pltpu.make_async_copy(freq_h, freq, lsem.at[6]),
        pltpu.make_async_copy(offset_h, offset, lsem.at[7]),
    ]
    for copy in local:
        copy.start()
    pl.semaphore_wait(barrier, n_z + n_h - 1)

    third_rows = LANES // 3
    odd = lax.rem(lo, 2)
    pair = hi * n_lo + lo + 1 - 2 * odd
    mine = pl.ds(pl.multiple_of(odd * third_rows, third_rows), third_rows)
    other = pl.ds(pl.multiple_of((1 - odd) * third_rows, third_rows), third_rows)
    both = pl.ds(2 * third_rows, third_rows)
    sends = []

    def send(*args):
        copy = remote(*args)
        copy.start()
        sends.append(copy)

    for e in range(1, n_h):
        send(qlat, qbuf.at[h], qs.at[e], qr.at[h], c, h_of[e])
    for d in range(n_z - 1, 0, -1):
        send(lat.at[mine, :], latbuf.at[c, mine, :], xzs.at[d], xzr.at[z], c_of[d], h)
    for d in range(n_z - 1, 0, -1):
        send(lat.at[both, :], latbuf.at[c, both, :], lzs.at[d], latr.at[c], c_of[d], h)
    send(lat, slot(c), lps.at[0], latr.at[c], partner, h)
    for d in range(1, n_z):
        send(tok_h, posbuf.at[k, z], pzs.at[d], pzr.at[z], c_of[d], h)
    for copy in local[5:]:
        copy.wait()
    posbuf[k, z] = tok[...]

    for d in range(1, n_z):
        cc = c_of[d]
        remote(lat.at[mine, :], latbuf.at[cc, mine, :], xzs.at[d], xzr.at[z_of[d]], cc, h).wait_recv()
        send(latbuf.at[cc, mine, :], latbuf.at[cc, mine, :], xps.at[d], xpr.at[z_of[d]], c, pair)

    positions = jnp.transpose(jnp.broadcast_to(tok[...].astype(F32), (8, rows)))[:, 0:1]
    absolute = jnp.transpose(jnp.broadcast_to((tok[...] + offset[...]).astype(F32), (8, rows)))[:, 0:1]
    angle = absolute * freq[...]
    cosine, sine = jnp.cos(angle), jnp.sin(angle)
    cos = jnp.concatenate([cosine, cosine], axis=1)
    sin = jnp.concatenate([-sine, sine], axis=1)

    local[0].wait()
    local[1].wait()
    for e in range(1, n_h):
        remote(qlat, qbuf.at[h_of[e]], qs.at[e], qr.at[h_of[e]], c, h_of[e]).wait_recv()
    query = None
    for g in range(n_h):
        term = jnp.dot(qbuf[g], wq_v[g * q_block:(g + 1) * q_block, :], preferred_element_type=F32)
        query = term if query is None else query + term
    local[2].wait()
    for j in range(heads):
        base = j * (NOPE + ROPE)
        nope = query[:, base:base + NOPE].astype(BF16)
        main = dot_t(nope, wkv_v[:, j * 256:j * 256 + NOPE])
        lines = slice(j * rows, (j + 1) * rows)
        qa[lines, 0:KVL] = main.astype(BF16)
        rope = query[:, base + NOPE:base + NOPE + ROPE]
        half = ROPE // 2
        swapped = jnp.concatenate([rope[:, half:], rope[:, :half]], axis=1)
        rotated = rope * cos + swapped * sin
        qa[lines, KVL:LANES] = rotated.astype(BF16)

    for d in range(1, n_z):
        cc = c_of[d]
        remote(lat.at[both, :], latbuf.at[cc, both, :], lzs.at[d], latr.at[cc], cc, h).wait_recv()
        remote(
            latbuf.at[cc, other, :], latbuf.at[cc, other, :], xps.at[d], xpr.at[z_of[d]], c, pair
        ).wait_recv()
        send(slot(c_of[d]), slot(c_of[d]), lps.at[d], latr.at[c_of[d]], partner, h)
    for d in range(1, n_z):
        remote(tok, posbuf.at[k, z_of[d]], pzs.at[d], pzr.at[z_of[d]], c_of[d], h).wait_recv()
    send(posbuf.at[k], posbuf.at[k], pps, ppr, partner, h)
    send(wout, w2.at[k], ws, wr, partner, h)
    local[3].wait()
    for d in range(n_z):
        cc = 2 * z_of[d] + 1 - k
        remote(lat, slot(cc), lps.at[d], latr.at[cc], partner, h).wait_recv()

    remote(posbuf.at[1 - k], posbuf.at[1 - k], pps, ppr, partner, h).wait_recv()
    key_pos = jnp.concatenate([posbuf[cc % 2, cc // 2] for cc in range(n_c)], axis=1).astype(F32)
    latents = jnp.concatenate([latbuf[cc] for cc in range(n_c)], axis=1)
    score[...] = jnp.dot(qa[...], latents, preferred_element_type=F32)
    visible = key_pos <= positions
    sums = []
    for j in range(heads):
        lines = slice(j * rows, (j + 1) * rows)
        s = jnp.where(visible, score[lines, :] * softmax_scale, negative_fill)
        largest = jnp.max(s, axis=-1, keepdims=True)
        weights = jnp.where(visible, jnp.exp(s - largest), 0.0)
        sums.append(jnp.sum(weights, axis=-1, keepdims=True))
        prob[lines, :] = weights.astype(BF16)
    summed = dot_t(prob[...], latents[0:KVL, :])
    for j in range(heads):
        normed = (summed[j * rows:(j + 1) * rows, :] / sums[j]).astype(BF16)
        value = jnp.dot(normed, wkv_v[:, j * 256 + NOPE:(j + 1) * 256], preferred_element_type=F32)
        attbuf[z, :, j * VDIM:(j + 1) * VDIM] = value.astype(BF16)

    for d in range(n_z - 1, 0, -1):
        send(attbuf.at[z], attbuf.at[z], ats.at[d], atr.at[z], c_of[d], h)

    local[4].wait()
    remote(wout, w2.at[1 - k], ws, wr, partner, h).wait_recv()

    def project(d):
        zz = z_of[d]
        if d > 0:
            remote(attbuf.at[zz], attbuf.at[zz], ats.at[d], atr.at[zz], c_of[d], h).wait_recv()
        part = jnp.dot(attbuf[zz], w2[0], preferred_element_type=F32).astype(BF16)
        for i in range(n_h):
            pa[d, i % n_lo, i // n_lo] = part[i * piece:(i + 1) * piece, :]
        for e in range(1, n_lo):
            send(pa.at[d, lo_of[e]], ra.at[d, lo], sa1.at[d, e], va1.at[d, lo], c, hi * n_lo + lo_of[e])
        part = jnp.dot(attbuf[zz], w2[1], preferred_element_type=F32).astype(BF16)
        for i in range(n_h):
            pb[d, i // n_lo, i % n_lo] = part[i * piece:(i + 1) * piece, :]
        send(pb.at[d, 1 - hi], rb.at[d], sb1.at[d], vb1.at[d], c, (1 - hi) * n_lo + lo)

    def second(d):
        total = pa[d, lo].astype(F32)
        for e in range(1, n_lo):
            ll = lo_of[e]
            remote(pa.at[d, ll], ra.at[d, ll], sa1.at[d, e], va1.at[d, ll], c, hi * n_lo + ll).wait_recv()
            total = total + ra[d, ll].astype(F32)
        ta[d] = total.astype(BF16)
        send(ta.at[d, 1 - hi], qa2.at[d], sa2.at[d], va2.at[d], c, (1 - hi) * n_lo + lo)
        remote(pb.at[d, hi], rb.at[d], sb1.at[d], vb1.at[d], c, (1 - hi) * n_lo + lo).wait_recv()
        tb[d] = (pb[d, hi].astype(F32) + rb[d].astype(F32)).astype(BF16)
        for e in range(1, n_lo):
            send(tb.at[d, lo_of[e]], qb2.at[d, lo], sb2.at[d, e], vb2.at[d, lo], c, hi * n_lo + lo_of[e])

    def third(d):
        remote(ta.at[d, hi], qa2.at[d], sa2.at[d], va2.at[d], c, (1 - hi) * n_lo + lo).wait_recv()
        first = (ta[d, hi].astype(F32) + qa2[d].astype(F32)).astype(BF16)
        total = tb[d, lo].astype(F32)
        for e in range(1, n_lo):
            ll = lo_of[e]
            remote(tb.at[d, ll], qb2.at[d, ll], sb2.at[d, e], vb2.at[d, ll], c, hi * n_lo + ll).wait_recv()
            total = total + qb2[d, ll].astype(F32)
        rbuf[d, :, 0:width] = first
        rbuf[d, :, width:] = total.astype(BF16)
        if d == 0:
            @pl.when(z != h)
            def _():
                deliver(d).start()

            @pl.when(z == h)
            def _():
                out[h] = rbuf[d]
        else:
            deliver(d).start()

    def deliver(d):
        return remote(rbuf.at[d], out.at[h], os_.at[d], or_.at[h], c_of[d], z)

    for d in range(n_z + 2):
        if d < n_z:
            project(d)
        if 1 <= d <= n_z:
            second(d - 1)
        if d >= 2:
            third(d - 2)
    for hh in range(n_h):
        @pl.when((z != h) | (h != hh))
        def _():
            remote(rbuf.at[0], out.at[hh], os_.at[0], or_.at[hh], c, h).wait_recv()
    for d in range(n_z):
        if d > 0:
            deliver(d).wait_send()
        else:
            @pl.when(z != h)
            def _():
                deliver(d).wait_send()
    for copy in sends:
        copy.wait_send()


def shards(n_c, n_h, q_latent, latent_cache, w_q_up, w_kv_up, w_out, token_pos, start_offset):
    rows, q_block = q_latent.shape
    heads = w_q_up.shape[1] // (NOPE + ROPE)
    n_z, n_lo = n_c // 2, n_h // 2
    assert n_z == n_h
    keys = n_c * rows
    width = w_out.shape[1]
    piece = rows // n_h
    freqs = rope_base ** (-np.arange(ROPE // 2) * 2.0 / ROPE)
    dma = pltpu.SemaphoreType.DMA
    anywhere = pl.BlockSpec(memory_space=pltpu.HBM)
    vmem = pl.BlockSpec(memory_space=pltpu.VMEM)
    result = pl.pallas_call(
        functools.partial(kernel, n_c, n_h, heads, rows),
        out_shape=pltpu.VMEM((n_h, piece, 2 * width), BF16),
        in_specs=[anywhere] * 8,
        out_specs=vmem,
        scratch_shapes=[
            pltpu.VMEM((1, rows), jnp.int32),
            pltpu.VMEM((1, ROPE // 2), F32),
            pltpu.VMEM((1, 1), jnp.int32),
            pltpu.VMEM(w_q_up.shape, BF16),
            pltpu.VMEM(w_kv_up.shape, BF16),
            pltpu.VMEM((2,) + w_out.shape, BF16),
            pltpu.VMEM((n_h, rows, q_block), BF16),
            pltpu.VMEM((n_c, LANES, rows), BF16),
            pltpu.VMEM((2, n_z, 1, rows), jnp.int32),
            pltpu.VMEM((heads * rows, LANES), BF16),
            pltpu.VMEM((heads * rows, keys), F32),
            pltpu.VMEM((heads * rows, keys), BF16),
            pltpu.VMEM((n_z, rows, heads * VDIM), BF16),
            pltpu.VMEM((n_z, n_lo, 2, piece, width), BF16),
            pltpu.VMEM((n_z, n_lo, 2, piece, width), BF16),
            pltpu.VMEM((n_z, 2, piece, width), BF16),
            pltpu.VMEM((n_z, piece, width), BF16),
            pltpu.VMEM((n_z, 2, n_lo, piece, width), BF16),
            pltpu.VMEM((n_z, n_lo, piece, width), BF16),
            pltpu.VMEM((n_z, n_lo, piece, width), BF16),
            pltpu.VMEM((n_z, n_lo, piece, width), BF16),
            pltpu.VMEM((n_z, piece, 2 * width), BF16),
            dma((8,)),
            dma((n_h,)), dma((n_h,)),
            dma((n_z,)), dma((n_z,)), dma((n_c,)),
            dma((n_z,)), dma((n_z,)), dma((n_z,)), dma((n_z,)),
            dma((n_z,)), dma((n_z,)), dma, dma,
            dma, dma,
            dma((n_z,)), dma((n_z,)),
            dma((n_z, n_lo)), dma((n_z, n_lo)), dma((n_z,)), dma((n_z,)),
            dma((n_z,)), dma((n_z,)), dma((n_z, n_lo)), dma((n_z, n_lo)),
            dma((n_z,)), dma((n_h,)),
        ],
        compiler_params=pltpu.CompilerParams(
            collective_id=0, has_side_effects=True, vmem_limit_bytes=67043328 - (768 << 10)
        ),
        name="mla",
    )(q_latent, latent_cache.T, w_q_up, w_kv_up, w_out, token_pos[None, :], freqs.astype(np.float32)[None, :], start_offset[None, :])
    return result.reshape(rows, 2 * width)


def solution(mesh):
    in_specs = (
        P("ctx", "head"),
        P("ctx", None),
        P(None, "head"),
        P(None, "head"),
        P("head", "ctx"),
        P("ctx"),
        P(),
    )
    out_specs = P("ctx", "head")
    body = functools.partial(shards, mesh.shape["ctx"], mesh.shape["head"])
    return jax.shard_map(body, mesh=mesh, in_specs=in_specs, out_specs=out_specs, check_vma=False)
```

```python
import functools

import jax
import jax.numpy as jnp
import numpy as np
from jax import lax
from jax.experimental import pallas as pl
from jax.experimental.pallas import tpu as pltpu
from jax.sharding import PartitionSpec as P

KVL = 512
NOPE = 128
ROPE = 64
VDIM = 128
LANES = KVL + ROPE

negative_fill = -1e30
softmax_scale = 0.135
rope_base = 10000.0
F32 = jnp.float32
BF16 = jnp.bfloat16
MESH = pl.DeviceIdType.MESH
gather_lag, reduce_lag = 4, 8


def dot_t(a, b):
    return lax.dot_general(a, b, (((1,), (1,)), ((), ())), preferred_element_type=F32)


def kernel(
    n_c, n_h, heads, rows, parts,
    qlat, lat, wq, wkv, wout, tok_h, freq_h, offset_h,
    out,
    tok, freq, offset, wq_v, wkv_v, w2, qbuf, latbuf, posbuf, qa, score, prob, attbuf,
    pa, ra, rbuf,
    lsem, qs, qr, lzs, lps, latr, xzs, xzr, xps, xpr, pzs, pzr, pps, ppr, ws, wr, ats, atr,
    gs, gr, rs, rr, os_, or_,
):
    n_z = n_c // 2
    n_lo = n_h // 2
    span = rows // parts
    piece = span // n_lo
    depth, width = wout.shape
    q_block = qbuf.shape[2]
    c = lax.axis_index("ctx")
    h = lax.axis_index("head")
    k = lax.rem(c, 2)
    z = lax.div(c, 2)
    partner = c + 1 - 2 * k
    z_of = [lax.rem(z + d, n_z) for d in range(n_z)]
    h_of = [lax.rem(h + e, n_h) for e in range(n_h)]
    shorter = jnp.minimum(z, n_z - 1 - z)
    slots = []
    for i in range(n_z):
        even = z - (i + 1) // 2 if i % 2 else z + i // 2
        single = jnp.where(2 * z < n_z, z + i - shorter, z - i + shorter)
        slots.append(jnp.where(i <= 2 * shorter, even, single))
    hi, lo = lax.div(h, n_lo), lax.rem(h, n_lo)
    lo_of = [lax.rem(lo + e, n_lo) for e in range(n_lo)]
    c_of = [2 * zz + k for zz in z_of]

    def remote(src, dst, ssem, rsem, cc, hh):
        return pltpu.make_async_remote_copy(
            src_ref=src, dst_ref=dst, send_sem=ssem, recv_sem=rsem,
            device_id=(cc, hh), device_id_type=MESH,
        )

    def slot(cc):
        return latbuf.at[cc]

    barrier = pltpu.get_barrier_semaphore()
    for d in range(1, n_z):
        pl.semaphore_signal(barrier, inc=1, device_id=(c_of[d], h), device_id_type=MESH)
    for e in range(1, n_h):
        pl.semaphore_signal(barrier, inc=1, device_id=(c, h_of[e]), device_id_type=MESH)
    pl.semaphore_signal(barrier, inc=1, device_id=(partner, h), device_id_type=MESH)

    local = [
        pltpu.make_async_copy(qlat, qbuf.at[h], lsem.at[0]),
        pltpu.make_async_copy(wq, wq_v, lsem.at[1]),
        pltpu.make_async_copy(wkv, wkv_v, lsem.at[2]),
        pltpu.make_async_copy(lat, slot(c), lsem.at[3]),
        pltpu.make_async_copy(tok_h, tok, lsem.at[4]),
        pltpu.make_async_copy(freq_h, freq, lsem.at[5]),
        pltpu.make_async_copy(offset_h, offset, lsem.at[6]),
    ]
    for copy in local:
        copy.start()
    keeps = k == hi
    across = (1 - hi) * n_lo + lo
    own_rows, other_rows = w2.at[0:depth, :], w2.at[depth:2 * depth, :]
    kept = pltpu.make_async_copy(wout, own_rows, lsem.at[7])
    pl.when(keeps)(kept.start)
    pl.semaphore_wait(barrier, n_z + n_h - 1)

    third_rows = LANES // 3
    odd = lax.rem(lo, 2)
    pair = hi * n_lo + lo + 1 - 2 * odd
    mine = pl.ds(pl.multiple_of(odd * third_rows, third_rows), third_rows)
    other = pl.ds(pl.multiple_of((1 - odd) * third_rows, third_rows), third_rows)
    both = pl.ds(2 * third_rows, third_rows)
    sends = []

    passed = []

    def send(*args):
        copy = remote(*args)
        copy.start()
        sends.append(copy)

    def start_if(ok, copy):
        pl.when(ok)(copy.start)
        passed.append((ok, copy))

    for e in range(1, n_h):
        send(qlat, qbuf.at[h], qs.at[e], qr.at[h], c, h_of[e])
    start_if(jnp.logical_not(keeps), remote(wout, other_rows, ws.at[0], wr.at[1], c, across))
    for d in range(n_z - 1, 0, -1):
        send(lat.at[mine, :], latbuf.at[c, mine, :], xzs.at[d], xzr.at[z], c_of[d], h)
    for d in range(n_z - 1, 0, -1):
        send(lat.at[both, :], latbuf.at[c, both, :], lzs.at[d], latr.at[c], c_of[d], h)
    send(lat, slot(c), lps.at[0], latr.at[c], partner, h)
    for d in range(1, n_z):
        send(tok_h, posbuf.at[k, z], pzs.at[d], pzr.at[z], c_of[d], h)
    for copy in local[4:]:
        copy.wait()
    posbuf[k, z] = tok[...]

    for d in range(1, n_z):
        cc = c_of[d]
        remote(lat.at[mine, :], latbuf.at[cc, mine, :], xzs.at[d], xzr.at[z_of[d]], cc, h).wait_recv()
        send(latbuf.at[cc, mine, :], latbuf.at[cc, mine, :], xps.at[d], xpr.at[z_of[d]], c, pair)

    positions = jnp.transpose(jnp.broadcast_to(tok[...].astype(F32), (8, rows)))[:, 0:1]
    absolute = jnp.transpose(jnp.broadcast_to((tok[...] + offset[0]).astype(F32), (8, rows)))[:, 0:1]
    angle = absolute * freq[...]
    cosine, sine = jnp.cos(angle), jnp.sin(angle)
    cos = jnp.concatenate([cosine, cosine], axis=1)
    sin = jnp.concatenate([-sine, sine], axis=1)

    local[0].wait()
    local[1].wait()
    for e in range(1, n_h):
        remote(qlat, qbuf.at[h_of[e]], qs.at[e], qr.at[h_of[e]], c, h_of[e]).wait_recv()
    query = None
    for g in range(n_h):
        term = jnp.dot(qbuf[g], wq_v[g * q_block:(g + 1) * q_block, :], preferred_element_type=F32)
        query = term if query is None else query + term
    local[2].wait()
    for j in range(heads):
        base = j * (NOPE + ROPE)
        nope = query[:, base:base + NOPE].astype(BF16)
        main = dot_t(nope, wkv_v[:, j * 256:j * 256 + NOPE])
        lines = slice(j * rows, (j + 1) * rows)
        qa[lines, 0:KVL] = main.astype(BF16)
        rope = query[:, base + NOPE:base + NOPE + ROPE]
        half = ROPE // 2
        swapped = jnp.concatenate([rope[:, half:], rope[:, :half]], axis=1)
        rotated = rope * cos + swapped * sin
        qa[lines, KVL:LANES] = rotated.astype(BF16)

    for d in range(1, n_z):
        cc = c_of[d]
        remote(lat.at[both, :], latbuf.at[cc, both, :], lzs.at[d], latr.at[cc], cc, h).wait_recv()
        remote(
            latbuf.at[cc, other, :], latbuf.at[cc, other, :], xps.at[d], xpr.at[z_of[d]], c, pair
        ).wait_recv()
        send(slot(c_of[d]), slot(c_of[d]), lps.at[d], latr.at[c_of[d]], partner, h)
    for d in range(1, n_z):
        remote(tok, posbuf.at[k, z_of[d]], pzs.at[d], pzr.at[z_of[d]], c_of[d], h).wait_recv()
    send(posbuf.at[k], posbuf.at[k], pps, ppr, partner, h)
    start_if(keeps, remote(wout, own_rows, ws.at[1], wr.at[0], partner, h))
    local[3].wait()
    for d in range(n_z):
        cc = 2 * z_of[d] + 1 - k
        remote(lat, slot(cc), lps.at[d], latr.at[cc], partner, h).wait_recv()

    remote(posbuf.at[1 - k], posbuf.at[1 - k], pps, ppr, partner, h).wait_recv()
    key_pos = jnp.concatenate([posbuf[cc % 2, cc // 2] for cc in range(n_c)], axis=1).astype(F32)
    latents = jnp.concatenate([latbuf[cc] for cc in range(n_c)], axis=1)
    score[...] = jnp.dot(qa[...], latents, preferred_element_type=F32)
    visible = key_pos <= positions
    sums = []
    for j in range(heads):
        lines = slice(j * rows, (j + 1) * rows)
        s = jnp.where(visible, score[lines, :] * softmax_scale, negative_fill)
        largest = jnp.max(s, axis=-1, keepdims=True)
        weights = jnp.where(visible, jnp.exp(s - largest), 0.0)
        sums.append(jnp.sum(weights, axis=-1, keepdims=True))
        prob[lines, :] = weights.astype(BF16)
    summed = dot_t(prob[...], latents[0:KVL, :])
    for j in range(heads):
        normed = (summed[j * rows:(j + 1) * rows, :] / sums[j]).astype(BF16)
        value = jnp.dot(normed, wkv_v[:, j * 256 + NOPE:(j + 1) * 256], preferred_element_type=F32)
        attbuf[z, :, j * VDIM:(j + 1) * VDIM] = value.astype(BF16)

    def pass_on(zz, p, row, to):
        lines = attbuf.at[zz, p * span:(p + 1) * span, 0:depth]
        return remote(lines, lines, ats.at[row, p], atr.at[zz, p], 2 * to + k, h)

    for p in range(parts):
        start_if(z + 1 < n_z, pass_on(z, p, 0, z + 1))
        start_if(z > 0, pass_on(z, p, n_z, z - 1))

    def share(d):
        zz, p = slots[d // parts], d % parts
        lines = attbuf.at[zz, p * span:(p + 1) * span, :]
        return remote(
            lines.at[:, 0:depth], lines.at[:, depth:2 * depth], gs.at[d], gr.at[d], c, across
        )

    def arrive(d):
        if d >= parts:
            zz, p = slots[d // parts], d % parts
            onward = jnp.where(zz < z, z + 1, z - 1)
            pass_on(zz, p, d // parts, z).wait_recv()
            start_if((onward >= 0) & (onward < n_z), pass_on(zz, p, d // parts, onward))
        share(d).start()

    def project(d):
        share(d).wait_recv()
        lines = attbuf[slots[d // parts], d % parts * span:(d % parts + 1) * span, :]
        part = jnp.dot(lines, w2[...], preferred_element_type=F32).astype(BF16)
        for i in range(n_lo):
            pa[d, i] = part[i * piece:(i + 1) * piece, :]
        for e in range(1, n_lo):
            send(pa.at[d, lo_of[e]], ra.at[d, lo], rs.at[d, e], rr.at[d, lo], c, hi * n_lo + lo_of[e])

    def place(side, p, line):
        if width % 128:
            return out.at[side, p, line]
        return out.at[p, line, :, pl.ds(pl.multiple_of(side * width, 128), width)]

    def deliver(d):
        return remote(
            rbuf.at[d], place(hi, d % parts, lo), os_.at[d], or_.at[d % parts, h],
            2 * slots[d // parts] + k, z,
        )

    def reduce(d):
        total = pa[d, lo].astype(F32)
        for e in range(1, n_lo):
            ll = lo_of[e]
            remote(pa.at[d, ll], ra.at[d, ll], rs.at[d, e], rr.at[d, ll], c, hi * n_lo + ll).wait_recv()
            total = total + ra[d, ll].astype(F32)
        rbuf[d] = total.astype(BF16)
        if d < parts:
            pl.when(z != h)(deliver(d).start)

            @pl.when(z == h)
            def _():
                place(hi, d % parts, lo)[...] = rbuf[d]
        else:
            deliver(d).start()

    def weights():
        @pl.when(keeps)
        def _():
            kept.wait()
            remote(wout, other_rows, ws.at[0], wr.at[1], c, across).wait_recv()

        start_if(keeps, remote(other_rows, other_rows, ws.at[2], wr.at[1], partner, h))

        @pl.when(jnp.logical_not(keeps))
        def _():
            remote(wout, own_rows, ws.at[1], wr.at[0], partner, h).wait_recv()
            remote(other_rows, other_rows, ws.at[2], wr.at[1], partner, h).wait_recv()

    chunks = n_z * parts
    for d in range(chunks + reduce_lag):
        if d < chunks:
            arrive(d)
        if d == gather_lag:
            weights()
        if 0 <= d - gather_lag < chunks:
            project(d - gather_lag)
        if 0 <= d - reduce_lag < chunks:
            reduce(d - reduce_lag)
    for hh in range(n_h):
        @pl.when((z != h) | (h != hh))
        def _():
            for p in range(parts):
                remote(
                    rbuf.at[0], place(hh // n_lo, p, hh % n_lo), os_.at[0], or_.at[p, hh], c, h
                ).wait_recv()
    for d in range(chunks):
        share(d).wait_send()
        if d >= parts:
            deliver(d).wait_send()
        else:
            pl.when(z != h)(deliver(d).wait_send)
    for ok, copy in passed:
        pl.when(ok)(copy.wait_send)
    for copy in sends:
        copy.wait_send()


def shards(n_c, n_h, q_latent, latent_cache, w_q_up, w_kv_up, w_out, token_pos, start_offset):
    rows, q_block = q_latent.shape
    heads = w_q_up.shape[1] // (NOPE + ROPE)
    n_z, n_lo = n_c // 2, n_h // 2
    assert n_z == n_h
    keys = n_c * rows
    width = w_out.shape[1]
    parts = 2 if rows // n_lo >= 32 else 1
    piece = rows // n_lo // parts
    chunks = n_z * parts
    split = 1 if width % 128 else 0
    freqs = rope_base ** (-np.arange(ROPE // 2) * 2.0 / ROPE)
    dma = pltpu.SemaphoreType.DMA
    anywhere = pl.BlockSpec(memory_space=pltpu.HBM)
    vmem = pl.BlockSpec(memory_space=pltpu.VMEM)
    result = pl.pallas_call(
        functools.partial(kernel, n_c, n_h, heads, rows, parts),
        out_shape=pltpu.VMEM((2,) * split + (parts, n_lo, piece, (2 - split) * width), BF16),
        in_specs=[anywhere] * 8,
        out_specs=vmem,
        scratch_shapes=[
            pltpu.VMEM((1, rows), jnp.int32),
            pltpu.VMEM((1, ROPE // 2), F32),
            pltpu.SMEM((1,), jnp.int32),
            pltpu.VMEM(w_q_up.shape, BF16),
            pltpu.VMEM(w_kv_up.shape, BF16),
            pltpu.VMEM((2 * w_out.shape[0], width), BF16),
            pltpu.VMEM((n_h, rows, q_block), BF16),
            pltpu.VMEM((n_c, LANES, rows), BF16),
            pltpu.VMEM((2, n_z, 1, rows), jnp.int32),
            pltpu.VMEM((heads * rows, LANES), BF16),
            pltpu.VMEM((heads * rows, keys), F32),
            pltpu.VMEM((heads * rows, keys), BF16),
            pltpu.VMEM((n_z, rows, 2 * heads * VDIM), BF16),
            pltpu.VMEM((chunks, n_lo, piece, width), BF16),
            pltpu.VMEM((chunks, n_lo, piece, width), BF16),
            pltpu.VMEM((chunks, piece, width), BF16),
            dma((8,)),
            dma((n_h,)), dma((n_h,)),
            dma((n_z,)), dma((n_z,)), dma((n_c,)),
            dma((n_z,)), dma((n_z,)), dma((n_z,)), dma((n_z,)),
            dma((n_z,)), dma((n_z,)), dma, dma,
            dma((3,)), dma((2,)),
            dma((n_z + 1, parts)), dma((n_z, parts)),
            dma((chunks,)), dma((chunks,)),
            dma((chunks, n_lo)), dma((chunks, n_lo)),
            dma((chunks,)), dma((parts, n_h)),
        ],
        compiler_params=pltpu.CompilerParams(
            collective_id=0, has_side_effects=True, vmem_limit_bytes=67043328 - (768 << 10)
        ),
        name="mla",
    )(q_latent, latent_cache.T, w_q_up, w_kv_up, w_out, token_pos[None, :], freqs.astype(np.float32)[None, :], start_offset)
    if not split:
        return result.reshape(rows, 2 * width)
    result = result.reshape(2, rows, width)
    return jnp.concatenate([result[0], result[1]], axis=1)


def solution(mesh):
    in_specs = (
        P("ctx", "head"),
        P("ctx", None),
        P(None, "head"),
        P(None, "head"),
        P("head", "ctx"),
        P("ctx"),
        P(),
    )
    out_specs = P("ctx", "head")
    body = functools.partial(shards, mesh.shape["ctx"], mesh.shape["head"])
    return jax.shard_map(body, mesh=mesh, in_specs=in_specs, out_specs=out_specs, check_vma=False)
```

```python
import functools

import jax
import jax.numpy as jnp
import numpy as np
from jax import lax
from jax.experimental import pallas as pl
from jax.experimental.pallas import tpu as pltpu
from jax.sharding import PartitionSpec as P

KVL = 512
NOPE = 128
ROPE = 64
VDIM = 128
LANES = KVL + ROPE

negative_fill = -1e30
softmax_scale = 0.135
rope_base = 10000.0
F32 = jnp.float32
BF16 = jnp.bfloat16
MESH = pl.DeviceIdType.MESH
strips, early_strips = 4, 1
gather_lag, reduce_lag = 4, 10


def dot_t(a, b):
    return lax.dot_general(a, b, (((1,), (1,)), ((), ())), preferred_element_type=F32)


def kernel(
    n_c, n_h, heads, rows, parts,
    qlat, lat, wq, wkv, wout, tok_h, freq_h, offset_h,
    out,
    tok, freq, offset, wq_v, wkv_v, w2, qbuf, latbuf, posbuf, qa, score, prob, attbuf,
    pa, ra, rbuf,
    lsem, qs, qr, lzs, lps, latr, xzs, xzr, xps, xpr, pzs, pzr, pps, ppr, ws, wr, ats, atr,
    gs, gr, rs, rr, os_, or_,
):
    n_z = n_c // 2
    n_lo = n_h // 2
    span = rows // parts
    piece = span // n_lo
    depth, width = wout.shape
    q_block = qbuf.shape[2]
    c = lax.axis_index("ctx")
    h = lax.axis_index("head")
    k = lax.rem(c, 2)
    z = lax.div(c, 2)
    partner = c + 1 - 2 * k
    z_of = [lax.rem(z + d, n_z) for d in range(n_z)]
    h_of = [lax.rem(h + e, n_h) for e in range(n_h)]
    shorter = jnp.minimum(z, n_z - 1 - z)
    slots = []
    for i in range(n_z):
        even = z - (i + 1) // 2 if i % 2 else z + i // 2
        single = jnp.where(2 * z < n_z, z + i - shorter, z - i + shorter)
        slots.append(jnp.where(i <= 2 * shorter, even, single))
    hi, lo = lax.div(h, n_lo), lax.rem(h, n_lo)
    lo_of = [lax.rem(lo + e, n_lo) for e in range(n_lo)]
    c_of = [2 * zz + k for zz in z_of]

    def remote(src, dst, ssem, rsem, cc, hh):
        return pltpu.make_async_remote_copy(
            src_ref=src, dst_ref=dst, send_sem=ssem, recv_sem=rsem,
            device_id=(cc, hh), device_id_type=MESH,
        )

    def slot(cc):
        return latbuf.at[cc]

    barrier = pltpu.get_barrier_semaphore()
    for d in range(1, n_z):
        pl.semaphore_signal(barrier, inc=1, device_id=(c_of[d], h), device_id_type=MESH)
    for e in range(1, n_h):
        pl.semaphore_signal(barrier, inc=1, device_id=(c, h_of[e]), device_id_type=MESH)
    pl.semaphore_signal(barrier, inc=1, device_id=(partner, h), device_id_type=MESH)

    local = [
        pltpu.make_async_copy(qlat, qbuf.at[h], lsem.at[0]),
        pltpu.make_async_copy(wq, wq_v, lsem.at[1]),
        pltpu.make_async_copy(wkv, wkv_v, lsem.at[2]),
        pltpu.make_async_copy(lat, slot(c), lsem.at[3]),
        pltpu.make_async_copy(tok_h, tok, lsem.at[4]),
        pltpu.make_async_copy(freq_h, freq, lsem.at[5]),
        pltpu.make_async_copy(offset_h, offset, lsem.at[6]),
    ]
    for copy in local:
        copy.start()
    keeps = k == hi
    across = (1 - hi) * n_lo + lo
    own_rows, other_rows = w2.at[0:depth, :], w2.at[depth:2 * depth, :]
    kept = pltpu.make_async_copy(wout, own_rows, lsem.at[7])
    pl.when(keeps)(kept.start)
    pl.semaphore_wait(barrier, n_z + n_h - 1)

    odd = lax.rem(lo, 2)
    beside = lo + 1 - 2 * odd
    peers = [(hi, beside), (1 - hi, lo), (1 - hi, beside)]
    share_rows = LANES // 36 * 6

    def part_of(a, b):
        return pl.ds(pl.multiple_of((2 * a + lax.rem(b, 2)) * share_rows, share_rows), share_rows)

    mine = part_of(hi, lo)
    both = pl.ds(4 * share_rows, LANES - 4 * share_rows)
    sends = []

    passed = []

    def send(*args):
        copy = remote(*args)
        copy.start()
        sends.append(copy)

    def start_if(ok, copy):
        pl.when(ok)(copy.start)
        passed.append((ok, copy))

    far = across
    send(qlat, qbuf.at[h], qs.at[0, 0], qr.at[h], c, far)
    for e in range(1, n_lo):
        send(qlat, qbuf.at[h], qs.at[0, e], qr.at[h], c, hi * n_lo + lo_of[e])

    def strip(i):
        return pl.ds(i * (depth // strips), depth // strips)

    def cross(i):
        return remote(
            wout.at[strip(i), :], other_rows.at[strip(i), :], ws.at[i], wr.at[1 + i], c, across
        )

    def hand_on(i):
        lines = other_rows.at[strip(i), :]
        pl.when(keeps)(cross(i).wait_recv)
        start_if(keeps, remote(lines, lines, ws.at[strips + i], wr.at[1 + i], partner, h))

    for i in range(early_strips):
        start_if(jnp.logical_not(keeps), cross(i))
    away = z_of[:0:-1]
    for i, zz in enumerate(away):
        send(lat.at[mine, :], latbuf.at[c, mine, :], xzs.at[i], xzr.at[z], 2 * zz + k, h)
    for i, zz in enumerate(away):
        send(lat.at[both, :], latbuf.at[c, both, :], lzs.at[i], latr.at[c], 2 * zz + k, h)
    send(lat, slot(c), lps.at[0], latr.at[c], partner, h)
    for i, zz in enumerate(away):
        send(tok_h, posbuf.at[k, z], pzs.at[i], pzr.at[z], 2 * zz + k, h)
    for copy in local[4:]:
        copy.wait()
    posbuf[k, z] = tok[...]

    remote(qlat, qbuf.at[far], qs.at[0, 0], qr.at[far], c, far).wait_recv()
    for e in range(1, n_lo):
        send(qbuf.at[far], qbuf.at[far], qs.at[1, e], qr.at[far], c, hi * n_lo + lo_of[e])

    for i in range(1, n_z):
        zz = z_of[i]
        cc = 2 * zz + k
        remote(lat.at[mine, :], latbuf.at[cc, mine, :], xzs.at[i - 1], xzr.at[zz], cc, h).wait_recv()
        for r, (a, b) in enumerate(peers):
            block = latbuf.at[cc, mine, :]
            send(block, block, xps.at[i, r], xpr.at[zz, r], c, a * n_lo + b)

    for i in range(early_strips, strips):
        start_if(jnp.logical_not(keeps), cross(i))

    positions = jnp.transpose(jnp.broadcast_to(tok[...].astype(F32), (8, rows)))[:, 0:1]
    absolute = jnp.transpose(jnp.broadcast_to((tok[...] + offset[0]).astype(F32), (8, rows)))[:, 0:1]
    angle = absolute * freq[...]
    cosine, sine = jnp.cos(angle), jnp.sin(angle)
    cos = jnp.concatenate([cosine, cosine], axis=1)
    sin = jnp.concatenate([-sine, sine], axis=1)

    local[0].wait()
    local[1].wait()
    for e in range(1, n_lo):
        for a in (hi, 1 - hi):
            there = a * n_lo + lo_of[e]
            remote(qlat, qbuf.at[there], qs.at[0, e], qr.at[there], c, there).wait_recv()
    query = None
    for g in range(n_h):
        term = jnp.dot(qbuf[g], wq_v[g * q_block:(g + 1) * q_block, :], preferred_element_type=F32)
        query = term if query is None else query + term
    local[2].wait()
    for j in range(heads):
        base = j * (NOPE + ROPE)
        nope = query[:, base:base + NOPE].astype(BF16)
        main = dot_t(nope, wkv_v[:, j * 256:j * 256 + NOPE])
        lines = slice(j * rows, (j + 1) * rows)
        qa[lines, 0:KVL] = main.astype(BF16)
        rope = query[:, base + NOPE:base + NOPE + ROPE]
        half = ROPE // 2
        swapped = jnp.concatenate([rope[:, half:], rope[:, :half]], axis=1)
        rotated = rope * cos + swapped * sin
        qa[lines, KVL:LANES] = rotated.astype(BF16)

    for i in range(1, n_z):
        zz = z_of[i]
        remote(tok, posbuf.at[k, zz], pzs.at[i - 1], pzr.at[zz], 2 * zz + k, h).wait_recv()
    send(posbuf.at[k], posbuf.at[k], pps, ppr, partner, h)
    for i in range(1, n_z):
        zz = z_of[i]
        cc = 2 * zz + k
        remote(lat.at[both, :], latbuf.at[cc, both, :], lzs.at[i - 1], latr.at[cc], cc, h).wait_recv()
        for r, (a, b) in enumerate(peers):
            block = latbuf.at[cc, part_of(a, b), :]
            remote(block, block, xps.at[i, r], xpr.at[zz, r], c, a * n_lo + b).wait_recv()
        send(slot(cc), slot(cc), lps.at[i], latr.at[cc], partner, h)
    start_if(keeps, remote(wout, own_rows, ws.at[2 * strips], wr.at[0], partner, h))
    local[3].wait()
    for i in range(n_z):
        cc = 2 * z_of[i] + 1 - k
        remote(lat, slot(cc), lps.at[i], latr.at[cc], partner, h).wait_recv()
    remote(posbuf.at[1 - k], posbuf.at[1 - k], pps, ppr, partner, h).wait_recv()
    for i in range(2):
        hand_on(i)
    key_pos = jnp.concatenate([posbuf[cc % 2, cc // 2] for cc in range(n_c)], axis=1).astype(F32)
    latents = jnp.concatenate([latbuf[cc] for cc in range(n_c)], axis=1)
    score[...] = jnp.dot(qa[...], latents, preferred_element_type=F32)
    visible = key_pos <= positions
    sums = []
    for j in range(heads):
        lines = slice(j * rows, (j + 1) * rows)
        s = jnp.where(visible, score[lines, :] * softmax_scale, negative_fill)
        largest = jnp.max(s, axis=-1, keepdims=True)
        weights = jnp.where(visible, jnp.exp(s - largest), 0.0)
        sums.append(jnp.sum(weights, axis=-1, keepdims=True))
        prob[lines, :] = weights.astype(BF16)
    summed = dot_t(prob[...], latents[0:KVL, :])
    for j in range(heads):
        normed = (summed[j * rows:(j + 1) * rows, :] / sums[j]).astype(BF16)
        value = jnp.dot(normed, wkv_v[:, j * 256 + NOPE:(j + 1) * 256], preferred_element_type=F32)
        attbuf[z, :, j * VDIM:(j + 1) * VDIM] = value.astype(BF16)

    def pass_on(zz, p, row, to):
        lines = attbuf.at[zz, p * span:(p + 1) * span, 0:depth]
        return remote(lines, lines, ats.at[row, p], atr.at[zz, p], 2 * to + k, h)

    for p in range(parts):
        start_if(z + 1 < n_z, pass_on(z, p, 0, z + 1))
        start_if(z > 0, pass_on(z, p, n_z, z - 1))

    def share(d):
        zz, p = slots[d // parts], d % parts
        lines = attbuf.at[zz, p * span:(p + 1) * span, :]
        return remote(
            lines.at[:, 0:depth], lines.at[:, depth:2 * depth], gs.at[d], gr.at[d], c, across
        )

    def arrive(d):
        if d >= parts:
            zz, p = slots[d // parts], d % parts
            onward = jnp.where(zz < z, z + 1, z - 1)
            pass_on(zz, p, d // parts, z).wait_recv()
            start_if((onward >= 0) & (onward < n_z), pass_on(zz, p, d // parts, onward))
        share(d).start()

    def project(d):
        share(d).wait_recv()
        lines = attbuf[slots[d // parts], d % parts * span:(d % parts + 1) * span, :]
        part = jnp.dot(lines, w2[...], preferred_element_type=F32).astype(BF16)
        for i in range(n_lo):
            pa[d, i] = part[i * piece:(i + 1) * piece, :]
        for e in range(1, n_lo):
            send(pa.at[d, lo_of[e]], ra.at[d, lo], rs.at[d, e], rr.at[d, lo], c, hi * n_lo + lo_of[e])

    def place(side, p, line):
        if width % 128:
            return out.at[side, p, line]
        return out.at[p, line, :, pl.ds(pl.multiple_of(side * width, 128), width)]

    def deliver(d):
        return remote(
            rbuf.at[d], place(hi, d % parts, lo), os_.at[d], or_.at[d % parts, h],
            2 * slots[d // parts] + k, z,
        )

    def reduce(d):
        total = pa[d, lo].astype(F32)
        for e in range(1, n_lo):
            ll = lo_of[e]
            remote(pa.at[d, ll], ra.at[d, ll], rs.at[d, e], rr.at[d, ll], c, hi * n_lo + ll).wait_recv()
            total = total + ra[d, ll].astype(F32)
        rbuf[d] = total.astype(BF16)
        if d < parts:
            pl.when(z != h)(deliver(d).start)

            @pl.when(z == h)
            def _():
                place(hi, d % parts, lo)[...] = rbuf[d]
        else:
            deliver(d).start()

    def weights():
        pl.when(keeps)(kept.wait)
        for i in range(2, strips):
            hand_on(i)

        @pl.when(jnp.logical_not(keeps))
        def _():
            remote(wout, own_rows, ws.at[2 * strips], wr.at[0], partner, h).wait_recv()
            for i in range(strips):
                lines = other_rows.at[strip(i), :]
                remote(lines, lines, ws.at[strips + i], wr.at[1 + i], partner, h).wait_recv()

    chunks = n_z * parts
    for d in range(chunks + reduce_lag):
        if d < chunks:
            arrive(d)
        if d == gather_lag:
            weights()
        if 0 <= d - gather_lag < chunks:
            project(d - gather_lag)
        if 0 <= d - reduce_lag < chunks:
            reduce(d - reduce_lag)
    for hh in range(n_h):
        @pl.when((z != h) | (h != hh))
        def _():
            for p in range(parts):
                remote(
                    rbuf.at[0], place(hh // n_lo, p, hh % n_lo), os_.at[0], or_.at[p, hh], c, h
                ).wait_recv()
    for d in range(chunks):
        share(d).wait_send()
        if d >= parts:
            deliver(d).wait_send()
        else:
            pl.when(z != h)(deliver(d).wait_send)
    for ok, copy in passed:
        pl.when(ok)(copy.wait_send)
    for copy in sends:
        copy.wait_send()


def shards(n_c, n_h, q_latent, latent_cache, w_q_up, w_kv_up, w_out, token_pos, start_offset):
    rows, q_block = q_latent.shape
    heads = w_q_up.shape[1] // (NOPE + ROPE)
    n_z, n_lo = n_c // 2, n_h // 2
    assert n_z == n_h
    keys = n_c * rows
    width = w_out.shape[1]
    parts = 2 if rows // n_lo >= 32 else 1
    piece = rows // n_lo // parts
    chunks = n_z * parts
    split = 1 if width % 128 else 0
    freqs = rope_base ** (-np.arange(ROPE // 2) * 2.0 / ROPE)
    dma = pltpu.SemaphoreType.DMA
    anywhere = pl.BlockSpec(memory_space=pltpu.HBM)
    vmem = pl.BlockSpec(memory_space=pltpu.VMEM)
    result = pl.pallas_call(
        functools.partial(kernel, n_c, n_h, heads, rows, parts),
        out_shape=pltpu.VMEM((2,) * split + (parts, n_lo, piece, (2 - split) * width), BF16),
        in_specs=[anywhere] * 8,
        out_specs=vmem,
        scratch_shapes=[
            pltpu.VMEM((1, rows), jnp.int32),
            pltpu.VMEM((1, ROPE // 2), F32),
            pltpu.SMEM((1,), jnp.int32),
            pltpu.VMEM(w_q_up.shape, BF16),
            pltpu.VMEM(w_kv_up.shape, BF16),
            pltpu.VMEM((2 * w_out.shape[0], width), BF16),
            pltpu.VMEM((n_h, rows, q_block), BF16),
            pltpu.VMEM((n_c, LANES, rows), BF16),
            pltpu.VMEM((2, n_z, 1, rows), jnp.int32),
            pltpu.VMEM((heads * rows, LANES), BF16),
            pltpu.VMEM((heads * rows, keys), F32),
            pltpu.VMEM((heads * rows, keys), BF16),
            pltpu.VMEM((n_z, rows, 2 * heads * VDIM), BF16),
            pltpu.VMEM((chunks, n_lo, piece, width), BF16),
            pltpu.VMEM((chunks, n_lo, piece, width), BF16),
            pltpu.VMEM((chunks, piece, width), BF16),
            dma((8,)),
            dma((2, n_lo)), dma((n_h,)),
            dma((n_z,)), dma((n_z,)), dma((n_c,)),
            dma((n_z,)), dma((n_z,)), dma((n_z, 3)), dma((n_z, 3)),
            dma((n_z,)), dma((n_z,)), dma, dma,
            dma((2 * strips + 1,)), dma((1 + strips,)),
            dma((n_z + 1, parts)), dma((n_z, parts)),
            dma((chunks,)), dma((chunks,)),
            dma((chunks, n_lo)), dma((chunks, n_lo)),
            dma((chunks,)), dma((parts, n_h)),
        ],
        compiler_params=pltpu.CompilerParams(
            collective_id=0, has_side_effects=True, vmem_limit_bytes=67043328 - (768 << 10)
        ),
        name="mla",
    )(q_latent, latent_cache.T, w_q_up, w_kv_up, w_out, token_pos[None, :], freqs.astype(np.float32)[None, :], start_offset)
    if not split:
        return result.reshape(rows, 2 * width)
    result = result.reshape(2, rows, width)
    return jnp.concatenate([result[0], result[1]], axis=1)


def solution(mesh):
    in_specs = (
        P("ctx", "head"),
        P("ctx", None),
        P(None, "head"),
        P(None, "head"),
        P("head", "ctx"),
        P("ctx"),
        P(),
    )
    out_specs = P("ctx", "head")
    body = functools.partial(shards, mesh.shape["ctx"], mesh.shape["head"])
    return jax.shard_map(body, mesh=mesh, in_specs=in_specs, out_specs=out_specs, check_vma=False)
```

```python
import functools

import jax
import jax.numpy as jnp
import numpy as np
from jax import lax
from jax.experimental import pallas as pl
from jax.experimental.pallas import tpu as pltpu
from jax.sharding import PartitionSpec as P

KVL = 512
NOPE = 128
ROPE = 64
VDIM = 128
LANES = KVL + ROPE

negative_fill = -1e30
softmax_scale = 0.135
rope_base = 10000.0
F32 = jnp.float32
BF16 = jnp.bfloat16
MESH = pl.DeviceIdType.MESH
strips, early_strips = 4, 1
gather_lag, reduce_lag = 4, 11


def dot_t(a, b):
    return lax.dot_general(a, b, (((1,), (1,)), ((), ())), preferred_element_type=F32)


def kernel(
    n_c, n_h, heads, rows, parts,
    qlat, lat, wq, wkv, wout, tok_h, freq_h, offset_h,
    out,
    tok, freq, offset, wq_v, wkv_v, w2, qbuf, latbuf, posbuf, qa, score, prob, attbuf,
    pa, ra, rbuf,
    lsem, qs, qr, lzs, lps, latr, xzs, xzr, xps, xpr, pzs, pzr, pps, ppr, ws, wr, ats, atr,
    gs, gr, rs, rr, os_, or_,
):
    n_z = n_c // 2
    n_lo = n_h // 2
    span = rows // parts
    piece = span // n_lo
    depth, width = wout.shape
    q_block = qbuf.shape[2]
    c = lax.axis_index("ctx")
    h = lax.axis_index("head")
    k = lax.rem(c, 2)
    z = lax.div(c, 2)
    partner = c + 1 - 2 * k
    z_of = [lax.rem(z + d, n_z) for d in range(n_z)]
    h_of = [lax.rem(h + e, n_h) for e in range(n_h)]
    shorter = jnp.minimum(z, n_z - 1 - z)
    slots = []
    for i in range(n_z):
        even = z - (i + 1) // 2 if i % 2 else z + i // 2
        single = jnp.where(2 * z < n_z, z + i - shorter, z - i + shorter)
        slots.append(jnp.where(i <= 2 * shorter, even, single))
    hi, lo = lax.div(h, n_lo), lax.rem(h, n_lo)
    lo_of = [lax.rem(lo + e, n_lo) for e in range(n_lo)]
    c_of = [2 * zz + k for zz in z_of]

    def remote(src, dst, ssem, rsem, cc, hh):
        return pltpu.make_async_remote_copy(
            src_ref=src, dst_ref=dst, send_sem=ssem, recv_sem=rsem,
            device_id=(cc, hh), device_id_type=MESH,
        )

    def slot(cc):
        return latbuf.at[cc]

    barrier = pltpu.get_barrier_semaphore()
    for d in range(1, n_z):
        pl.semaphore_signal(barrier, inc=1, device_id=(c_of[d], h), device_id_type=MESH)
    for e in range(1, n_h):
        pl.semaphore_signal(barrier, inc=1, device_id=(c, h_of[e]), device_id_type=MESH)
    pl.semaphore_signal(barrier, inc=1, device_id=(partner, h), device_id_type=MESH)

    local = [
        pltpu.make_async_copy(qlat, qbuf.at[h], lsem.at[0]),
        pltpu.make_async_copy(wq, wq_v, lsem.at[1]),
        pltpu.make_async_copy(wkv, wkv_v, lsem.at[2]),
        pltpu.make_async_copy(lat, slot(c), lsem.at[3]),
        pltpu.make_async_copy(tok_h, tok, lsem.at[4]),
        pltpu.make_async_copy(freq_h, freq, lsem.at[5]),
        pltpu.make_async_copy(offset_h, offset, lsem.at[6]),
    ]
    for copy in local:
        copy.start()
    keeps = k == hi
    across = (1 - hi) * n_lo + lo
    own_rows, other_rows = w2.at[0:depth, :], w2.at[depth:2 * depth, :]
    kept = pltpu.make_async_copy(wout, own_rows, lsem.at[7])
    pl.when(keeps)(kept.start)
    pl.semaphore_wait(barrier, n_z + n_h - 1)

    odd = lax.rem(lo, 2)
    beside = lo + 1 - 2 * odd
    peers = [(hi, beside), (1 - hi, lo), (1 - hi, beside)]
    share_rows = LANES // 36 * 5

    def part_of(a, b):
        return pl.ds(pl.multiple_of((2 * a + lax.rem(b, 2)) * share_rows, share_rows), share_rows)

    mine = part_of(hi, lo)
    both = pl.ds(4 * share_rows, LANES - 4 * share_rows)
    sends = []

    passed = []

    def send(*args):
        copy = remote(*args)
        copy.start()
        sends.append(copy)

    def start_if(ok, copy):
        pl.when(ok)(copy.start)
        passed.append((ok, copy))

    far = across
    send(qlat, qbuf.at[h], qs.at[0, 0], qr.at[h], c, far)
    for e in range(1, n_lo):
        send(qlat, qbuf.at[h], qs.at[0, e], qr.at[h], c, hi * n_lo + lo_of[e])

    def strip(i):
        return pl.ds(i * (depth // strips), depth // strips)

    def cross(i):
        return remote(
            wout.at[strip(i), :], other_rows.at[strip(i), :], ws.at[i], wr.at[1 + i], c, across
        )

    def hand_on(i):
        lines = other_rows.at[strip(i), :]
        pl.when(keeps)(cross(i).wait_recv)
        start_if(keeps, remote(lines, lines, ws.at[strips + i], wr.at[1 + i], partner, h))

    for i in range(early_strips):
        start_if(jnp.logical_not(keeps), cross(i))
    away = z_of[:0:-1]
    for i, zz in enumerate(away):
        send(lat.at[mine, :], latbuf.at[c, mine, :], xzs.at[i], xzr.at[z], 2 * zz + k, h)
    for i, zz in enumerate(away):
        send(lat.at[both, :], latbuf.at[c, both, :], lzs.at[i], latr.at[c], 2 * zz + k, h)
    send(lat, slot(c), lps.at[0], latr.at[c], partner, h)
    for i, zz in enumerate(away):
        send(tok_h, posbuf.at[k, z], pzs.at[i], pzr.at[z], 2 * zz + k, h)
    for copy in local[4:]:
        copy.wait()
    posbuf[k, z] = tok[...]

    remote(qlat, qbuf.at[far], qs.at[0, 0], qr.at[far], c, far).wait_recv()
    for e in range(1, n_lo):
        send(qbuf.at[far], qbuf.at[far], qs.at[1, e], qr.at[far], c, hi * n_lo + lo_of[e])

    for i in range(1, n_z):
        zz = z_of[i]
        cc = 2 * zz + k
        remote(lat.at[mine, :], latbuf.at[cc, mine, :], xzs.at[i - 1], xzr.at[zz], cc, h).wait_recv()
        for r, (a, b) in enumerate(peers):
            block = latbuf.at[cc, mine, :]
            send(block, block, xps.at[i, r], xpr.at[zz, r], c, a * n_lo + b)

    for i in range(early_strips, strips):
        start_if(jnp.logical_not(keeps), cross(i))

    positions = jnp.transpose(jnp.broadcast_to(tok[...].astype(F32), (8, rows)))[:, 0:1]
    absolute = jnp.transpose(jnp.broadcast_to((tok[...] + offset[0]).astype(F32), (8, rows)))[:, 0:1]
    angle = absolute * freq[...]
    cosine, sine = jnp.cos(angle), jnp.sin(angle)
    cos = jnp.concatenate([cosine, cosine], axis=1)
    sin = jnp.concatenate([-sine, sine], axis=1)

    local[0].wait()
    local[1].wait()
    for e in range(1, n_lo):
        for a in (hi, 1 - hi):
            there = a * n_lo + lo_of[e]
            remote(qlat, qbuf.at[there], qs.at[0, e], qr.at[there], c, there).wait_recv()
    query = None
    for g in range(n_h):
        term = jnp.dot(qbuf[g], wq_v[g * q_block:(g + 1) * q_block, :], preferred_element_type=F32)
        query = term if query is None else query + term
    local[2].wait()
    for j in range(heads):
        base = j * (NOPE + ROPE)
        nope = query[:, base:base + NOPE].astype(BF16)
        main = dot_t(nope, wkv_v[:, j * 256:j * 256 + NOPE])
        lines = slice(j * rows, (j + 1) * rows)
        qa[lines, 0:KVL] = main.astype(BF16)
        rope = query[:, base + NOPE:base + NOPE + ROPE]
        half = ROPE // 2
        swapped = jnp.concatenate([rope[:, half:], rope[:, :half]], axis=1)
        rotated = rope * cos + swapped * sin
        qa[lines, KVL:LANES] = rotated.astype(BF16)

    for i in range(1, n_z):
        zz = z_of[i]
        cc = 2 * zz + k
        remote(lat.at[both, :], latbuf.at[cc, both, :], lzs.at[i - 1], latr.at[cc], cc, h).wait_recv()
        for r, (a, b) in enumerate(peers):
            block = latbuf.at[cc, part_of(a, b), :]
            remote(block, block, xps.at[i, r], xpr.at[zz, r], c, a * n_lo + b).wait_recv()
        send(slot(cc), slot(cc), lps.at[i], latr.at[cc], partner, h)
    for i in range(1, n_z):
        zz = z_of[i]
        remote(tok, posbuf.at[k, zz], pzs.at[i - 1], pzr.at[zz], 2 * zz + k, h).wait_recv()
    send(posbuf.at[k], posbuf.at[k], pps, ppr, partner, h)
    start_if(keeps, remote(wout, own_rows, ws.at[2 * strips], wr.at[0], partner, h))
    local[3].wait()
    for i in range(n_z):
        cc = 2 * z_of[i] + 1 - k
        remote(lat, slot(cc), lps.at[i], latr.at[cc], partner, h).wait_recv()
    remote(posbuf.at[1 - k], posbuf.at[1 - k], pps, ppr, partner, h).wait_recv()
    for i in range(2):
        hand_on(i)
    key_pos = jnp.concatenate([posbuf[cc % 2, cc // 2] for cc in range(n_c)], axis=1).astype(F32)
    latents = jnp.concatenate([latbuf[cc] for cc in range(n_c)], axis=1)
    score[...] = jnp.dot(qa[...], latents, preferred_element_type=F32)
    visible = key_pos <= positions
    sums = []
    for j in range(heads):
        lines = slice(j * rows, (j + 1) * rows)
        s = jnp.where(visible, score[lines, :] * softmax_scale, negative_fill)
        largest = jnp.max(s, axis=-1, keepdims=True)
        weights = jnp.exp(s - largest)
        sums.append(jnp.sum(weights, axis=-1, keepdims=True))
        prob[lines, :] = weights.astype(BF16)
    summed = dot_t(prob[...], latents[0:KVL, :])
    for j in range(heads):
        normed = (summed[j * rows:(j + 1) * rows, :] / sums[j]).astype(BF16)
        value = jnp.dot(normed, wkv_v[:, j * 256 + NOPE:(j + 1) * 256], preferred_element_type=F32)
        attbuf[z, :, j * VDIM:(j + 1) * VDIM] = value.astype(BF16)

    def pass_on(zz, p, row, to):
        lines = attbuf.at[zz, p * span:(p + 1) * span, 0:depth]
        return remote(lines, lines, ats.at[row, p], atr.at[zz, p], 2 * to + k, h)

    for p in range(parts):
        start_if(z + 1 < n_z, pass_on(z, p, 0, z + 1))
        start_if(z > 0, pass_on(z, p, n_z, z - 1))

    def share(d):
        zz, p = slots[d // parts], d % parts
        lines = attbuf.at[zz, p * span:(p + 1) * span, :]
        return remote(
            lines.at[:, 0:depth], lines.at[:, depth:2 * depth], gs.at[d], gr.at[d], c, across
        )

    def arrive(d):
        if d >= parts:
            zz, p = slots[d // parts], d % parts
            onward = jnp.where(zz < z, z + 1, z - 1)
            pass_on(zz, p, d // parts, z).wait_recv()
            start_if((onward >= 0) & (onward < n_z), pass_on(zz, p, d // parts, onward))
        share(d).start()

    def project(d):
        share(d).wait_recv()
        lines = attbuf[slots[d // parts], d % parts * span:(d % parts + 1) * span, :]
        part = jnp.dot(lines, w2[...], preferred_element_type=F32).astype(BF16)
        for i in range(n_lo):
            pa[d, i] = part[i * piece:(i + 1) * piece, :]
        for e in range(1, n_lo):
            send(pa.at[d, lo_of[e]], ra.at[d, lo], rs.at[d, e], rr.at[d, lo], c, hi * n_lo + lo_of[e])

    def place(side, p, line):
        if width % 128:
            return out.at[side, p, line]
        return out.at[p, line, :, pl.ds(pl.multiple_of(side * width, 128), width)]

    def deliver(d):
        return remote(
            rbuf.at[d], place(hi, d % parts, lo), os_.at[d], or_.at[d % parts, h],
            2 * slots[d // parts] + k, z,
        )

    def reduce(d):
        total = pa[d, lo].astype(F32)
        for e in range(1, n_lo):
            ll = lo_of[e]
            remote(pa.at[d, ll], ra.at[d, ll], rs.at[d, e], rr.at[d, ll], c, hi * n_lo + ll).wait_recv()
            total = total + ra[d, ll].astype(F32)
        rbuf[d] = total.astype(BF16)
        if d < parts:
            pl.when(z != h)(deliver(d).start)

            @pl.when(z == h)
            def _():
                place(hi, d % parts, lo)[...] = rbuf[d]
        else:
            deliver(d).start()

    def weights():
        pl.when(keeps)(kept.wait)
        for i in range(2, strips):
            hand_on(i)

        @pl.when(jnp.logical_not(keeps))
        def _():
            remote(wout, own_rows, ws.at[2 * strips], wr.at[0], partner, h).wait_recv()
            for i in range(strips):
                lines = other_rows.at[strip(i), :]
                remote(lines, lines, ws.at[strips + i], wr.at[1 + i], partner, h).wait_recv()

    chunks = n_z * parts
    for d in range(chunks + reduce_lag):
        if d < chunks:
            arrive(d)
        if d == gather_lag:
            weights()
        if 0 <= d - gather_lag < chunks:
            project(d - gather_lag)
        if 0 <= d - reduce_lag < chunks:
            reduce(d - reduce_lag)
    for hh in range(n_h):
        @pl.when((z != h) | (h != hh))
        def _():
            for p in range(parts):
                remote(
                    rbuf.at[0], place(hh // n_lo, p, hh % n_lo), os_.at[0], or_.at[p, hh], c, h
                ).wait_recv()
    for d in range(chunks):
        share(d).wait_send()
        if d >= parts:
            deliver(d).wait_send()
        else:
            pl.when(z != h)(deliver(d).wait_send)
    for ok, copy in passed:
        pl.when(ok)(copy.wait_send)
    for copy in sends:
        copy.wait_send()


def shards(n_c, n_h, q_latent, latent_cache, w_q_up, w_kv_up, w_out, token_pos, start_offset):
    rows, q_block = q_latent.shape
    heads = w_q_up.shape[1] // (NOPE + ROPE)
    n_z, n_lo = n_c // 2, n_h // 2
    assert n_z == n_h
    keys = n_c * rows
    width = w_out.shape[1]
    parts = 2 if rows // n_lo >= 32 else 1
    piece = rows // n_lo // parts
    chunks = n_z * parts
    split = 1 if width % 128 else 0
    freqs = rope_base ** (-np.arange(ROPE // 2) * 2.0 / ROPE)
    dma = pltpu.SemaphoreType.DMA
    anywhere = pl.BlockSpec(memory_space=pltpu.HBM)
    vmem = pl.BlockSpec(memory_space=pltpu.VMEM)
    result = pl.pallas_call(
        functools.partial(kernel, n_c, n_h, heads, rows, parts),
        out_shape=pltpu.VMEM((2,) * split + (parts, n_lo, piece, (2 - split) * width), BF16),
        in_specs=[anywhere] * 8,
        out_specs=vmem,
        scratch_shapes=[
            pltpu.VMEM((1, rows), jnp.int32),
            pltpu.VMEM((1, ROPE // 2), F32),
            pltpu.SMEM((1,), jnp.int32),
            pltpu.VMEM(w_q_up.shape, BF16),
            pltpu.VMEM(w_kv_up.shape, BF16),
            pltpu.VMEM((2 * w_out.shape[0], width), BF16),
            pltpu.VMEM((n_h, rows, q_block), BF16),
            pltpu.VMEM((n_c, LANES, rows), BF16),
            pltpu.VMEM((2, n_z, 1, rows), jnp.int32),
            pltpu.VMEM((heads * rows, LANES), BF16),
            pltpu.VMEM((heads * rows, keys), F32),
            pltpu.VMEM((heads * rows, keys), BF16),
            pltpu.VMEM((n_z, rows, 2 * heads * VDIM), BF16),
            pltpu.VMEM((chunks, n_lo, piece, width), BF16),
            pltpu.VMEM((chunks, n_lo, piece, width), BF16),
            pltpu.VMEM((chunks, piece, width), BF16),
            dma((8,)),
            dma((2, n_lo)), dma((n_h,)),
            dma((n_z,)), dma((n_z,)), dma((n_c,)),
            dma((n_z,)), dma((n_z,)), dma((n_z, 3)), dma((n_z, 3)),
            dma((n_z,)), dma((n_z,)), dma, dma,
            dma((2 * strips + 1,)), dma((1 + strips,)),
            dma((n_z + 1, parts)), dma((n_z, parts)),
            dma((chunks,)), dma((chunks,)),
            dma((chunks, n_lo)), dma((chunks, n_lo)),
            dma((chunks,)), dma((parts, n_h)),
        ],
        compiler_params=pltpu.CompilerParams(
            collective_id=0, has_side_effects=True, vmem_limit_bytes=67043328 - (768 << 10)
        ),
        name="mla",
    )(q_latent, latent_cache.T, w_q_up, w_kv_up, w_out, token_pos[None, :], freqs.astype(np.float32)[None, :], start_offset)
    if not split:
        return result.reshape(rows, 2 * width)
    result = result.reshape(2, rows, width)
    return jnp.concatenate([result[0], result[1]], axis=1)


def solution(mesh):
    in_specs = (
        P("ctx", "head"),
        P("ctx", None),
        P(None, "head"),
        P(None, "head"),
        P("head", "ctx"),
        P("ctx"),
        P(),
    )
    out_specs = P("ctx", "head")
    body = functools.partial(shards, mesh.shape["ctx"], mesh.shape["head"])
    return jax.shard_map(body, mesh=mesh, in_specs=in_specs, out_specs=out_specs, check_vma=False)
```

```python
import functools

import jax
import jax.numpy as jnp
import numpy as np
from jax import lax
from jax.experimental import pallas as pl
from jax.experimental.pallas import tpu as pltpu
from jax.sharding import PartitionSpec as P

KVL = 512
NOPE = 128
ROPE = 64
VDIM = 128
LANES = KVL + ROPE

negative_fill = -1e30
softmax_scale = 0.135
rope_base = 10000.0
F32 = jnp.float32
BF16 = jnp.bfloat16
MESH = pl.DeviceIdType.MESH
strips, early_strips = 4, 1
gather_lag, reduce_lag = 4, 11


def dot_t(a, b):
    return lax.dot_general(a, b, (((1,), (1,)), ((), ())), preferred_element_type=F32)


def kernel(
    n_c, n_h, heads, rows, parts,
    qlat, lat, wq, wkv, wout, tok_h, freq_h, offset_h,
    out,
    tok, freq, offset, wq_v, wkv_v, w2, qbuf, latbuf, posbuf, qa, score, prob, attbuf,
    pa, ra, rbuf,
    lsem, qs, qr, lzs, lps, latr, xzs, xzr, xps, xpr, pzs, pzr, pps, ppr, ws, wr, ats, atr,
    gs, gr, rs, rr, os_, or_,
):
    n_z = n_c // 2
    n_lo = n_h // 2
    span = rows // parts
    piece = span // n_lo
    depth, width = wout.shape
    q_block = qbuf.shape[2]
    c = lax.axis_index("ctx")
    h = lax.axis_index("head")
    k = lax.rem(c, 2)
    z = lax.div(c, 2)
    partner = c + 1 - 2 * k
    z_of = [lax.rem(z + d, n_z) for d in range(n_z)]
    h_of = [lax.rem(h + e, n_h) for e in range(n_h)]
    shorter = jnp.minimum(z, n_z - 1 - z)
    slots = []
    for i in range(n_z):
        even = z - (i + 1) // 2 if i % 2 else z + i // 2
        single = jnp.where(2 * z < n_z, z + i - shorter, z - i + shorter)
        slots.append(jnp.where(i <= 2 * shorter, even, single))
    hi, lo = lax.div(h, n_lo), lax.rem(h, n_lo)
    lo_of = [lax.rem(lo + e, n_lo) for e in range(n_lo)]
    c_of = [2 * zz + k for zz in z_of]

    def remote(src, dst, ssem, rsem, cc, hh):
        return pltpu.make_async_remote_copy(
            src_ref=src, dst_ref=dst, send_sem=ssem, recv_sem=rsem,
            device_id=(cc, hh), device_id_type=MESH,
        )

    def slot(cc):
        return latbuf.at[cc]

    barrier = pltpu.get_barrier_semaphore()
    for d in range(1, n_z):
        pl.semaphore_signal(barrier, inc=1, device_id=(c_of[d], h), device_id_type=MESH)
    for e in range(1, n_h):
        pl.semaphore_signal(barrier, inc=1, device_id=(c, h_of[e]), device_id_type=MESH)
    pl.semaphore_signal(barrier, inc=1, device_id=(partner, h), device_id_type=MESH)

    local = [
        pltpu.make_async_copy(qlat, qbuf.at[h], lsem.at[0]),
        pltpu.make_async_copy(wq, wq_v, lsem.at[1]),
        pltpu.make_async_copy(wkv, wkv_v, lsem.at[2]),
        pltpu.make_async_copy(lat, slot(c), lsem.at[3]),
        pltpu.make_async_copy(tok_h, tok, lsem.at[4]),
        pltpu.make_async_copy(freq_h, freq, lsem.at[5]),
        pltpu.make_async_copy(offset_h, offset, lsem.at[6]),
    ]
    for copy in local:
        copy.start()
    keeps = k == hi
    across = (1 - hi) * n_lo + lo
    own_rows, other_rows = w2.at[0:depth, :], w2.at[depth:2 * depth, :]
    kept = pltpu.make_async_copy(wout, own_rows, lsem.at[7])
    pl.when(keeps)(kept.start)
    pl.semaphore_wait(barrier, n_z + n_h - 1)

    odd = lax.rem(lo, 2)
    beside = lo + 1 - 2 * odd
    peers = [(hi, beside), (1 - hi, lo), (1 - hi, beside)]
    share_rows = LANES // 36 * 5

    def part_of(a, b):
        return pl.ds(pl.multiple_of((2 * a + lax.rem(b, 2)) * share_rows, share_rows), share_rows)

    mine = part_of(hi, lo)
    both = pl.ds(4 * share_rows, LANES - 4 * share_rows)
    sends = []

    passed = []

    def send(*args):
        copy = remote(*args)
        copy.start()
        sends.append(copy)

    def start_if(ok, copy):
        pl.when(ok)(copy.start)
        passed.append((ok, copy))

    far = across
    send(lat, slot(c), lps.at[0], latr.at[c], partner, h)
    send(qlat, qbuf.at[h], qs.at[0, 0], qr.at[h], c, far)
    for e in range(1, n_lo):
        send(qlat, qbuf.at[h], qs.at[0, e], qr.at[h], c, hi * n_lo + lo_of[e])

    def strip(i):
        return pl.ds(i * (depth // strips), depth // strips)

    def cross(i):
        return remote(
            wout.at[strip(i), :], other_rows.at[strip(i), :], ws.at[i], wr.at[1 + i], c, across
        )

    def hand_on(i):
        lines = other_rows.at[strip(i), :]
        pl.when(keeps)(cross(i).wait_recv)
        start_if(keeps, remote(lines, lines, ws.at[strips + i], wr.at[1 + i], partner, h))

    for i in range(early_strips):
        start_if(jnp.logical_not(keeps), cross(i))
    away = slots[1:]
    for i, zz in enumerate(away):
        send(lat.at[mine, :], latbuf.at[c, mine, :], xzs.at[i], xzr.at[z], 2 * zz + k, h)
    for i, zz in enumerate(away):
        send(lat.at[both, :], latbuf.at[c, both, :], lzs.at[i], latr.at[c], 2 * zz + k, h)
    for i, zz in enumerate(away):
        send(tok_h, posbuf.at[k, z], pzs.at[i], pzr.at[z], 2 * zz + k, h)
    for copy in local[4:]:
        copy.wait()
    posbuf[k, z] = tok[...]

    remote(qlat, qbuf.at[far], qs.at[0, 0], qr.at[far], c, far).wait_recv()
    for e in range(1, n_lo):
        send(qbuf.at[far], qbuf.at[far], qs.at[1, e], qr.at[far], c, hi * n_lo + lo_of[e])

    for i in range(1, n_z):
        zz = slots[i]
        cc = 2 * zz + k
        remote(lat.at[mine, :], latbuf.at[cc, mine, :], xzs.at[i - 1], xzr.at[zz], cc, h).wait_recv()
        for r, (a, b) in enumerate(peers):
            block = latbuf.at[cc, mine, :]
            send(block, block, xps.at[i, r], xpr.at[zz, r], c, a * n_lo + b)

    for i in range(early_strips, strips):
        start_if(jnp.logical_not(keeps), cross(i))

    positions = jnp.transpose(jnp.broadcast_to(tok[...].astype(F32), (8, rows)))[:, 0:1]
    absolute = jnp.transpose(jnp.broadcast_to((tok[...] + offset[0]).astype(F32), (8, rows)))[:, 0:1]
    angle = absolute * freq[...]
    cosine, sine = jnp.cos(angle), jnp.sin(angle)
    cos = jnp.concatenate([cosine, cosine], axis=1)
    sin = jnp.concatenate([-sine, sine], axis=1)

    local[0].wait()
    local[1].wait()
    for e in range(1, n_lo):
        for a in (hi, 1 - hi):
            there = a * n_lo + lo_of[e]
            remote(qlat, qbuf.at[there], qs.at[0, e], qr.at[there], c, there).wait_recv()
    query = None
    for g in range(n_h):
        term = jnp.dot(qbuf[g], wq_v[g * q_block:(g + 1) * q_block, :], preferred_element_type=F32)
        query = term if query is None else query + term
    local[2].wait()
    for j in range(heads):
        base = j * (NOPE + ROPE)
        nope = query[:, base:base + NOPE].astype(BF16)
        main = dot_t(nope, wkv_v[:, j * 256:j * 256 + NOPE])
        rope = query[:, base + NOPE:base + NOPE + ROPE]
        half = ROPE // 2
        swapped = jnp.concatenate([rope[:, half:], rope[:, :half]], axis=1)
        rotated = rope * cos + swapped * sin
        for p in range(parts):
            lines = slice((p * heads + j) * span, (p * heads + j + 1) * span)
            qa[lines, 0:KVL] = main[p * span:(p + 1) * span].astype(BF16)
            qa[lines, KVL:LANES] = rotated[p * span:(p + 1) * span].astype(BF16)

    for i in range(1, n_z):
        zz = slots[i]
        cc = 2 * zz + k
        remote(lat.at[both, :], latbuf.at[cc, both, :], lzs.at[i - 1], latr.at[cc], cc, h).wait_recv()
        for r, (a, b) in enumerate(peers):
            block = latbuf.at[cc, part_of(a, b), :]
            remote(block, block, xps.at[i, r], xpr.at[zz, r], c, a * n_lo + b).wait_recv()
        send(slot(cc), slot(cc), lps.at[i], latr.at[cc], partner, h)
    for i in range(1, n_z):
        zz = slots[i]
        remote(tok, posbuf.at[k, zz], pzs.at[i - 1], pzr.at[zz], 2 * zz + k, h).wait_recv()
    send(posbuf.at[k], posbuf.at[k], pps, ppr, partner, h)
    start_if(keeps, remote(wout, own_rows, ws.at[2 * strips], wr.at[0], partner, h))
    local[3].wait()
    for i in range(n_z):
        cc = 2 * slots[i] + 1 - k
        remote(lat, slot(cc), lps.at[i], latr.at[cc], partner, h).wait_recv()
    remote(posbuf.at[1 - k], posbuf.at[1 - k], pps, ppr, partner, h).wait_recv()
    for i in range(2):
        hand_on(i)
    key_pos = jnp.concatenate([posbuf[cc % 2, cc // 2] for cc in range(n_c)], axis=1).astype(F32)
    latents = jnp.concatenate([latbuf[cc] for cc in range(n_c)], axis=1)
    def pass_on(zz, p, row, to):
        lines = attbuf.at[zz, p * span:(p + 1) * span, 0:depth]
        return remote(lines, lines, ats.at[row, p], atr.at[zz, p], 2 * to + k, h)

    def share(d):
        zz, p = slots[d // parts], d % parts
        lines = attbuf.at[zz, p * span:(p + 1) * span, :]
        return remote(
            lines.at[:, 0:depth], lines.at[:, depth:2 * depth], gs.at[d], gr.at[d], c, across
        )

    score[...] = jnp.dot(qa[...], latents, preferred_element_type=F32)
    for p in range(parts):
        visible = key_pos <= positions[p * span:(p + 1) * span]
        sums = []
        for j in range(heads):
            lines = slice((p * heads + j) * span, (p * heads + j + 1) * span)
            s = jnp.where(visible, score[lines, :] * softmax_scale, negative_fill)
            largest = jnp.max(s, axis=-1, keepdims=True)
            weights = jnp.exp(s - largest)
            sums.append(jnp.sum(weights, axis=-1, keepdims=True))
            prob[lines, :] = weights.astype(BF16)
        lines = slice(p * heads * span, (p + 1) * heads * span)
        summed = dot_t(prob[lines, :], latents[0:KVL, :])
        for j in range(heads):
            normed = (summed[j * span:(j + 1) * span, :] / sums[j]).astype(BF16)
            value = jnp.dot(normed, wkv_v[:, j * 256 + NOPE:(j + 1) * 256], preferred_element_type=F32)
            attbuf[z, p * span:(p + 1) * span, j * VDIM:(j + 1) * VDIM] = value.astype(BF16)
        start_if(z + 1 < n_z, pass_on(z, p, 0, z + 1))
        start_if(z > 0, pass_on(z, p, n_z, z - 1))
        share(p).start()

    def arrive(d):
        if d >= parts:
            zz, p = slots[d // parts], d % parts
            onward = jnp.where(zz < z, z + 1, z - 1)
            pass_on(zz, p, d // parts, z).wait_recv()
            start_if((onward >= 0) & (onward < n_z), pass_on(zz, p, d // parts, onward))
            share(d).start()

    def project(d):
        share(d).wait_recv()
        lines = attbuf[slots[d // parts], d % parts * span:(d % parts + 1) * span, :]
        part = jnp.dot(lines, w2[...], preferred_element_type=F32).astype(BF16)
        for i in range(n_lo):
            pa[d, i] = part[i * piece:(i + 1) * piece, :]
        for e in range(1, n_lo):
            send(pa.at[d, lo_of[e]], ra.at[d, lo], rs.at[d, e], rr.at[d, lo], c, hi * n_lo + lo_of[e])

    def place(side, p, line):
        if width % 128:
            return out.at[side, p, line]
        return out.at[p, line, :, pl.ds(pl.multiple_of(side * width, 128), width)]

    def deliver(d):
        return remote(
            rbuf.at[d], place(hi, d % parts, lo), os_.at[d], or_.at[d % parts, h],
            2 * slots[d // parts] + k, z,
        )

    def reduce(d):
        total = pa[d, lo].astype(F32)
        for e in range(1, n_lo):
            ll = lo_of[e]
            remote(pa.at[d, ll], ra.at[d, ll], rs.at[d, e], rr.at[d, ll], c, hi * n_lo + ll).wait_recv()
            total = total + ra[d, ll].astype(F32)
        rbuf[d] = total.astype(BF16)
        if d < parts:
            pl.when(z != h)(deliver(d).start)

            @pl.when(z == h)
            def _():
                place(hi, d % parts, lo)[...] = rbuf[d]
        else:
            deliver(d).start()

    def weights():
        pl.when(keeps)(kept.wait)
        for i in range(2, strips):
            hand_on(i)

        @pl.when(jnp.logical_not(keeps))
        def _():
            remote(wout, own_rows, ws.at[2 * strips], wr.at[0], partner, h).wait_recv()
            for i in range(strips):
                lines = other_rows.at[strip(i), :]
                remote(lines, lines, ws.at[strips + i], wr.at[1 + i], partner, h).wait_recv()

    chunks = n_z * parts
    for d in range(chunks + reduce_lag):
        if d < chunks:
            arrive(d)
        if d == gather_lag:
            weights()
        if 0 <= d - gather_lag < chunks:
            project(d - gather_lag)
        if 0 <= d - reduce_lag < chunks:
            reduce(d - reduce_lag)
    for hh in range(n_h):
        @pl.when((z != h) | (h != hh))
        def _():
            for p in range(parts):
                remote(
                    rbuf.at[0], place(hh // n_lo, p, hh % n_lo), os_.at[0], or_.at[p, hh], c, h
                ).wait_recv()
    for d in range(chunks):
        share(d).wait_send()
        if d >= parts:
            deliver(d).wait_send()
        else:
            pl.when(z != h)(deliver(d).wait_send)
    for ok, copy in passed:
        pl.when(ok)(copy.wait_send)
    for copy in sends:
        copy.wait_send()


def shards(n_c, n_h, q_latent, latent_cache, w_q_up, w_kv_up, w_out, token_pos, start_offset):
    rows, q_block = q_latent.shape
    heads = w_q_up.shape[1] // (NOPE + ROPE)
    n_z, n_lo = n_c // 2, n_h // 2
    assert n_z == n_h
    keys = n_c * rows
    width = w_out.shape[1]
    parts = 2 if rows // n_lo >= 32 else 1
    piece = rows // n_lo // parts
    chunks = n_z * parts
    split = 1 if width % 128 else 0
    freqs = rope_base ** (-np.arange(ROPE // 2) * 2.0 / ROPE)
    dma = pltpu.SemaphoreType.DMA
    anywhere = pl.BlockSpec(memory_space=pltpu.HBM)
    vmem = pl.BlockSpec(memory_space=pltpu.VMEM)
    result = pl.pallas_call(
        functools.partial(kernel, n_c, n_h, heads, rows, parts),
        out_shape=pltpu.VMEM((2,) * split + (parts, n_lo, piece, (2 - split) * width), BF16),
        in_specs=[anywhere] * 8,
        out_specs=vmem,
        scratch_shapes=[
            pltpu.VMEM((1, rows), jnp.int32),
            pltpu.VMEM((1, ROPE // 2), F32),
            pltpu.SMEM((1,), jnp.int32),
            pltpu.VMEM(w_q_up.shape, BF16),
            pltpu.VMEM(w_kv_up.shape, BF16),
            pltpu.VMEM((2 * w_out.shape[0], width), BF16),
            pltpu.VMEM((n_h, rows, q_block), BF16),
            pltpu.VMEM((n_c, LANES, rows), BF16),
            pltpu.VMEM((2, n_z, 1, rows), jnp.int32),
            pltpu.VMEM((heads * rows, LANES), BF16),
            pltpu.VMEM((heads * rows, keys), F32),
            pltpu.VMEM((heads * rows, keys), BF16),
            pltpu.VMEM((n_z, rows, 2 * heads * VDIM), BF16),
            pltpu.VMEM((chunks, n_lo, piece, width), BF16),
            pltpu.VMEM((chunks, n_lo, piece, width), BF16),
            pltpu.VMEM((chunks, piece, width), BF16),
            dma((8,)),
            dma((2, n_lo)), dma((n_h,)),
            dma((n_z,)), dma((n_z,)), dma((n_c,)),
            dma((n_z,)), dma((n_z,)), dma((n_z, 3)), dma((n_z, 3)),
            dma((n_z,)), dma((n_z,)), dma, dma,
            dma((2 * strips + 1,)), dma((1 + strips,)),
            dma((n_z + 1, parts)), dma((n_z, parts)),
            dma((chunks,)), dma((chunks,)),
            dma((chunks, n_lo)), dma((chunks, n_lo)),
            dma((chunks,)), dma((parts, n_h)),
        ],
        compiler_params=pltpu.CompilerParams(
            collective_id=0, has_side_effects=True, vmem_limit_bytes=67043328 - (768 << 10)
        ),
        name="mla",
    )(q_latent, latent_cache.T, w_q_up, w_kv_up, w_out, token_pos[None, :], freqs.astype(np.float32)[None, :], start_offset)
    if not split:
        return result.reshape(rows, 2 * width)
    result = result.reshape(2, rows, width)
    return jnp.concatenate([result[0], result[1]], axis=1)


def solution(mesh):
    in_specs = (
        P("ctx", "head"),
        P("ctx", None),
        P(None, "head"),
        P(None, "head"),
        P("head", "ctx"),
        P("ctx"),
        P(),
    )
    out_specs = P("ctx", "head")
    body = functools.partial(shards, mesh.shape["ctx"], mesh.shape["head"])
    return jax.shard_map(body, mesh=mesh, in_specs=in_specs, out_specs=out_specs, check_vma=False)
```

```python
import functools

import jax
import jax.numpy as jnp
import numpy as np
from jax import lax
from jax.experimental import pallas as pl
from jax.experimental.pallas import tpu as pltpu
from jax.sharding import PartitionSpec as P

KVL = 512
NOPE = 128
ROPE = 64
VDIM = 128
LANES = KVL + ROPE

negative_fill = -1e30
softmax_scale = 0.135
rope_base = 10000.0
F32 = jnp.float32
BF16 = jnp.bfloat16
MESH = pl.DeviceIdType.MESH
strips, early_strips = 4, 1
gather_lag, reduce_lag = 4, 11


def dot_t(a, b):
    return lax.dot_general(a, b, (((1,), (1,)), ((), ())), preferred_element_type=F32)


def kernel(
    n_c, n_h, heads, rows, parts,
    qlat, lat, wq, wkv, wout, tok_h, freq_h, offset_h,
    out,
    tok, freq, offset, wq_v, wkv_v, w2, qbuf, latbuf, posbuf, qa, score, prob, attbuf,
    pa, ra, rbuf,
    lsem, qs, qr, lzs, lps, latr, xzs, xzr, xps, xpr, pzs, pzr, pps, ppr, ws, wr, ats, atr,
    gs, gr, rs, rr, os_, or_,
):
    n_z = n_c // 2
    n_lo = n_h // 2
    span = rows // parts
    piece = span // n_lo
    depth, width = wout.shape
    q_block = qbuf.shape[2]
    c = lax.axis_index("ctx")
    h = lax.axis_index("head")
    k = lax.rem(c, 2)
    z = lax.div(c, 2)
    partner = c + 1 - 2 * k
    z_of = [lax.rem(z + d, n_z) for d in range(n_z)]
    h_of = [lax.rem(h + e, n_h) for e in range(n_h)]
    shorter = jnp.minimum(z, n_z - 1 - z)
    slots = []
    for i in range(n_z):
        even = z - (i + 1) // 2 if i % 2 else z + i // 2
        single = jnp.where(2 * z < n_z, z + i - shorter, z - i + shorter)
        slots.append(jnp.where(i <= 2 * shorter, even, single))
    hi, lo = lax.div(h, n_lo), lax.rem(h, n_lo)
    lo_of = [lax.rem(lo + e, n_lo) for e in range(n_lo)]
    c_of = [2 * zz + k for zz in z_of]

    def remote(src, dst, ssem, rsem, cc, hh):
        return pltpu.make_async_remote_copy(
            src_ref=src, dst_ref=dst, send_sem=ssem, recv_sem=rsem,
            device_id=(cc, hh), device_id_type=MESH,
        )

    def slot(cc):
        return latbuf.at[cc]

    barrier = pltpu.get_barrier_semaphore()
    for d in range(1, n_z):
        pl.semaphore_signal(barrier, inc=1, device_id=(c_of[d], h), device_id_type=MESH)
    for e in range(1, n_h):
        pl.semaphore_signal(barrier, inc=1, device_id=(c, h_of[e]), device_id_type=MESH)
    pl.semaphore_signal(barrier, inc=1, device_id=(partner, h), device_id_type=MESH)

    local = [
        pltpu.make_async_copy(qlat, qbuf.at[h], lsem.at[0]),
        pltpu.make_async_copy(wq, wq_v, lsem.at[1]),
        pltpu.make_async_copy(wkv, wkv_v, lsem.at[2]),
        pltpu.make_async_copy(lat, slot(c), lsem.at[3]),
        pltpu.make_async_copy(tok_h, tok, lsem.at[4]),
        pltpu.make_async_copy(freq_h, freq, lsem.at[5]),
        pltpu.make_async_copy(offset_h, offset, lsem.at[6]),
    ]
    for copy in local:
        copy.start()
    keeps = k == hi
    across = (1 - hi) * n_lo + lo
    own_rows, other_rows = w2.at[0:depth, :], w2.at[depth:2 * depth, :]
    kept = pltpu.make_async_copy(wout, own_rows, lsem.at[7])
    pl.when(keeps)(kept.start)
    pl.semaphore_wait(barrier, n_z + n_h - 1)

    odd = lax.rem(lo, 2)
    beside = lo + 1 - 2 * odd
    peers = [(hi, beside), (1 - hi, lo), (1 - hi, beside)]
    share_rows = LANES // 36 * 5

    def part_of(a, b):
        return pl.ds(pl.multiple_of((2 * a + lax.rem(b, 2)) * share_rows, share_rows), share_rows)

    mine = part_of(hi, lo)
    both = pl.ds(4 * share_rows, LANES - 4 * share_rows)
    sends = []

    passed = []

    def send(*args):
        copy = remote(*args)
        copy.start()
        sends.append(copy)

    def start_if(ok, copy):
        pl.when(ok)(copy.start)
        passed.append((ok, copy))

    far = across
    send(lat, slot(c), lps.at[0], latr.at[c], partner, h)
    send(qlat, qbuf.at[h], qs.at[0, 0], qr.at[h], c, far)
    for e in range(1, n_lo):
        send(qlat, qbuf.at[h], qs.at[0, e], qr.at[h], c, hi * n_lo + lo_of[e])

    def strip(i):
        return pl.ds(i * (depth // strips), depth // strips)

    def cross(i):
        return remote(
            wout.at[strip(i), :], other_rows.at[strip(i), :], ws.at[i], wr.at[1 + i], c, across
        )

    def hand_on(i):
        lines = other_rows.at[strip(i), :]
        pl.when(keeps)(cross(i).wait_recv)
        start_if(keeps, remote(lines, lines, ws.at[strips + i], wr.at[1 + i], partner, h))

    for i in range(early_strips):
        start_if(jnp.logical_not(keeps), cross(i))
    away = slots[1:]
    for i, zz in enumerate(away):
        send(lat.at[mine, :], latbuf.at[c, mine, :], xzs.at[i], xzr.at[z], 2 * zz + k, h)
    for i, zz in enumerate(away):
        send(lat.at[both, :], latbuf.at[c, both, :], lzs.at[i], latr.at[c], 2 * zz + k, h)
    for i, zz in enumerate(away):
        send(tok_h, posbuf.at[k, z], pzs.at[i], pzr.at[z], 2 * zz + k, h)
    for copy in local[4:]:
        copy.wait()
    posbuf[k, z] = tok[...]

    remote(qlat, qbuf.at[far], qs.at[0, 0], qr.at[far], c, far).wait_recv()
    for e in range(1, n_lo):
        send(qbuf.at[far], qbuf.at[far], qs.at[1, e], qr.at[far], c, hi * n_lo + lo_of[e])

    for i in range(1, n_z):
        zz = slots[i]
        cc = 2 * zz + k
        remote(lat.at[mine, :], latbuf.at[cc, mine, :], xzs.at[i - 1], xzr.at[zz], cc, h).wait_recv()
        for r, (a, b) in enumerate(peers):
            block = latbuf.at[cc, mine, :]
            send(block, block, xps.at[i, r], xpr.at[zz, r], c, a * n_lo + b)

    for i in range(early_strips, strips):
        start_if(jnp.logical_not(keeps), cross(i))

    start_if(keeps, remote(wout, own_rows, ws.at[2 * strips], wr.at[0], partner, h))

    positions = jnp.transpose(jnp.broadcast_to(tok[...].astype(F32), (8, rows)))[:, 0:1]
    absolute = jnp.transpose(jnp.broadcast_to((tok[...] + offset[0]).astype(F32), (8, rows)))[:, 0:1]
    angle = absolute * freq[...]
    cosine, sine = jnp.cos(angle), jnp.sin(angle)
    cos = jnp.concatenate([cosine, cosine], axis=1)
    sin = jnp.concatenate([-sine, sine], axis=1)

    local[0].wait()
    local[1].wait()
    for e in range(1, n_lo):
        for a in (hi, 1 - hi):
            there = a * n_lo + lo_of[e]
            remote(qlat, qbuf.at[there], qs.at[0, e], qr.at[there], c, there).wait_recv()
    query = None
    for g in range(n_h):
        term = jnp.dot(qbuf[g], wq_v[g * q_block:(g + 1) * q_block, :], preferred_element_type=F32)
        query = term if query is None else query + term
    local[2].wait()
    for j in range(heads):
        base = j * (NOPE + ROPE)
        nope = query[:, base:base + NOPE].astype(BF16)
        main = dot_t(nope, wkv_v[:, j * 256:j * 256 + NOPE])
        rope = query[:, base + NOPE:base + NOPE + ROPE]
        half = ROPE // 2
        swapped = jnp.concatenate([rope[:, half:], rope[:, :half]], axis=1)
        rotated = rope * cos + swapped * sin
        for p in range(parts):
            lines = slice((p * heads + j) * span, (p * heads + j + 1) * span)
            qa[lines, 0:KVL] = main[p * span:(p + 1) * span].astype(BF16)
            qa[lines, KVL:LANES] = rotated[p * span:(p + 1) * span].astype(BF16)

    for i in range(1, n_z):
        zz = slots[i]
        cc = 2 * zz + k
        remote(lat.at[both, :], latbuf.at[cc, both, :], lzs.at[i - 1], latr.at[cc], cc, h).wait_recv()
        for r, (a, b) in enumerate(peers):
            block = latbuf.at[cc, part_of(a, b), :]
            remote(block, block, xps.at[i, r], xpr.at[zz, r], c, a * n_lo + b).wait_recv()
        send(slot(cc), slot(cc), lps.at[i], latr.at[cc], partner, h)
    for i in range(1, n_z):
        zz = slots[i]
        remote(tok, posbuf.at[k, zz], pzs.at[i - 1], pzr.at[zz], 2 * zz + k, h).wait_recv()
    send(posbuf.at[k], posbuf.at[k], pps, ppr, partner, h)
    local[3].wait()
    for i in range(n_z):
        cc = 2 * slots[i] + 1 - k
        remote(lat, slot(cc), lps.at[i], latr.at[cc], partner, h).wait_recv()
    remote(posbuf.at[1 - k], posbuf.at[1 - k], pps, ppr, partner, h).wait_recv()
    for i in range(2):
        hand_on(i)
    key_pos = jnp.concatenate([posbuf[cc % 2, cc // 2] for cc in range(n_c)], axis=1).astype(F32)
    latents = jnp.concatenate([latbuf[cc] for cc in range(n_c)], axis=1)
    def pass_on(zz, p, row, to):
        lines = attbuf.at[zz, p * span:(p + 1) * span, 0:depth]
        return remote(lines, lines, ats.at[row, p], atr.at[zz, p], 2 * to + k, h)

    def share(d):
        zz, p = slots[d // parts], d % parts
        lines = attbuf.at[zz, p * span:(p + 1) * span, :]
        return remote(
            lines.at[:, 0:depth], lines.at[:, depth:2 * depth], gs.at[d], gr.at[d], c, across
        )

    score[...] = jnp.dot(qa[...], latents, preferred_element_type=F32)
    for p in range(parts):
        visible = key_pos <= positions[p * span:(p + 1) * span]
        sums = []
        for j in range(heads):
            lines = slice((p * heads + j) * span, (p * heads + j + 1) * span)
            s = jnp.where(visible, score[lines, :] * softmax_scale, negative_fill)
            largest = jnp.max(s, axis=-1, keepdims=True)
            weights = jnp.exp(s - largest)
            sums.append(jnp.sum(weights, axis=-1, keepdims=True))
            prob[lines, :] = weights.astype(BF16)
        lines = slice(p * heads * span, (p + 1) * heads * span)
        summed = dot_t(prob[lines, :], latents[0:KVL, :])
        for j in range(heads):
            normed = (summed[j * span:(j + 1) * span, :] / sums[j]).astype(BF16)
            value = jnp.dot(normed, wkv_v[:, j * 256 + NOPE:(j + 1) * 256], preferred_element_type=F32)
            attbuf[z, p * span:(p + 1) * span, j * VDIM:(j + 1) * VDIM] = value.astype(BF16)
        start_if(z + 1 < n_z, pass_on(z, p, 0, z + 1))
        start_if(z > 0, pass_on(z, p, n_z, z - 1))
        share(p).start()

    def arrive(d):
        if d >= parts:
            zz, p = slots[d // parts], d % parts
            onward = jnp.where(zz < z, z + 1, z - 1)
            pass_on(zz, p, d // parts, z).wait_recv()
            start_if((onward >= 0) & (onward < n_z), pass_on(zz, p, d // parts, onward))
            share(d).start()

    def project(d):
        share(d).wait_recv()
        lines = attbuf[slots[d // parts], d % parts * span:(d % parts + 1) * span, :]
        part = jnp.dot(lines, w2[...], preferred_element_type=F32).astype(BF16)
        for i in range(n_lo):
            pa[d, i] = part[i * piece:(i + 1) * piece, :]
        for e in range(1, n_lo):
            send(pa.at[d, lo_of[e]], ra.at[d, lo], rs.at[d, e], rr.at[d, lo], c, hi * n_lo + lo_of[e])

    def place(side, p, line):
        if width % 128:
            return out.at[side, p, line]
        return out.at[p, line, :, pl.ds(pl.multiple_of(side * width, 128), width)]

    def deliver(d):
        return remote(
            rbuf.at[d], place(hi, d % parts, lo), os_.at[d], or_.at[d % parts, h],
            2 * slots[d // parts] + k, z,
        )

    def reduce(d):
        total = pa[d, lo].astype(F32)
        for e in range(1, n_lo):
            ll = lo_of[e]
            remote(pa.at[d, ll], ra.at[d, ll], rs.at[d, e], rr.at[d, ll], c, hi * n_lo + ll).wait_recv()
            total = total + ra[d, ll].astype(F32)
        rbuf[d] = total.astype(BF16)
        if d < parts:
            pl.when(z != h)(deliver(d).start)

            @pl.when(z == h)
            def _():
                place(hi, d % parts, lo)[...] = rbuf[d]
        else:
            deliver(d).start()

    def weights():
        pl.when(keeps)(kept.wait)
        for i in range(2, strips):
            hand_on(i)

        @pl.when(jnp.logical_not(keeps))
        def _():
            remote(wout, own_rows, ws.at[2 * strips], wr.at[0], partner, h).wait_recv()
            for i in range(strips):
                lines = other_rows.at[strip(i), :]
                remote(lines, lines, ws.at[strips + i], wr.at[1 + i], partner, h).wait_recv()

    chunks = n_z * parts
    for d in range(chunks + reduce_lag):
        if d < chunks:
            arrive(d)
        if d == gather_lag:
            weights()
        if 0 <= d - gather_lag < chunks:
            project(d - gather_lag)
        if 0 <= d - reduce_lag < chunks:
            reduce(d - reduce_lag)
    for hh in range(n_h):
        @pl.when((z != h) | (h != hh))
        def _():
            for p in range(parts):
                remote(
                    rbuf.at[0], place(hh // n_lo, p, hh % n_lo), os_.at[0], or_.at[p, hh], c, h
                ).wait_recv()
    for d in range(chunks):
        share(d).wait_send()
        if d >= parts:
            deliver(d).wait_send()
        else:
            pl.when(z != h)(deliver(d).wait_send)
    for ok, copy in passed:
        pl.when(ok)(copy.wait_send)
    for copy in sends:
        copy.wait_send()


def shards(n_c, n_h, q_latent, latent_cache, w_q_up, w_kv_up, w_out, token_pos, start_offset):
    rows, q_block = q_latent.shape
    heads = w_q_up.shape[1] // (NOPE + ROPE)
    n_z, n_lo = n_c // 2, n_h // 2
    assert n_z == n_h
    keys = n_c * rows
    width = w_out.shape[1]
    parts = 2 if rows // n_lo >= 32 else 1
    piece = rows // n_lo // parts
    chunks = n_z * parts
    split = 1 if width % 128 else 0
    freqs = rope_base ** (-np.arange(ROPE // 2) * 2.0 / ROPE)
    dma = pltpu.SemaphoreType.DMA
    anywhere = pl.BlockSpec(memory_space=pltpu.HBM)
    vmem = pl.BlockSpec(memory_space=pltpu.VMEM)
    result = pl.pallas_call(
        functools.partial(kernel, n_c, n_h, heads, rows, parts),
        out_shape=pltpu.VMEM((2,) * split + (parts, n_lo, piece, (2 - split) * width), BF16),
        in_specs=[anywhere] * 8,
        out_specs=vmem,
        scratch_shapes=[
            pltpu.VMEM((1, rows), jnp.int32),
            pltpu.VMEM((1, ROPE // 2), F32),
            pltpu.SMEM((1,), jnp.int32),
            pltpu.VMEM(w_q_up.shape, BF16),
            pltpu.VMEM(w_kv_up.shape, BF16),
            pltpu.VMEM((2 * w_out.shape[0], width), BF16),
            pltpu.VMEM((n_h, rows, q_block), BF16),
            pltpu.VMEM((n_c, LANES, rows), BF16),
            pltpu.VMEM((2, n_z, 1, rows), jnp.int32),
            pltpu.VMEM((heads * rows, LANES), BF16),
            pltpu.VMEM((heads * rows, keys), F32),
            pltpu.VMEM((heads * rows, keys), BF16),
            pltpu.VMEM((n_z, rows, 2 * heads * VDIM), BF16),
            pltpu.VMEM((chunks, n_lo, piece, width), BF16),
            pltpu.VMEM((chunks, n_lo, piece, width), BF16),
            pltpu.VMEM((chunks, piece, width), BF16),
            dma((8,)),
            dma((2, n_lo)), dma((n_h,)),
            dma((n_z,)), dma((n_z,)), dma((n_c,)),
            dma((n_z,)), dma((n_z,)), dma((n_z, 3)), dma((n_z, 3)),
            dma((n_z,)), dma((n_z,)), dma, dma,
            dma((2 * strips + 1,)), dma((1 + strips,)),
            dma((n_z + 1, parts)), dma((n_z, parts)),
            dma((chunks,)), dma((chunks,)),
            dma((chunks, n_lo)), dma((chunks, n_lo)),
            dma((chunks,)), dma((parts, n_h)),
        ],
        compiler_params=pltpu.CompilerParams(
            collective_id=0, has_side_effects=True, vmem_limit_bytes=67043328 - (768 << 10)
        ),
        name="mla",
    )(q_latent, latent_cache.T, w_q_up, w_kv_up, w_out, token_pos[None, :], freqs.astype(np.float32)[None, :], start_offset)
    if not split:
        return result.reshape(rows, 2 * width)
    result = result.reshape(2, rows, width)
    return jnp.concatenate([result[0], result[1]], axis=1)


def solution(mesh):
    in_specs = (
        P("ctx", "head"),
        P("ctx", None),
        P(None, "head"),
        P(None, "head"),
        P("head", "ctx"),
        P("ctx"),
        P(),
    )
    out_specs = P("ctx", "head")
    body = functools.partial(shards, mesh.shape["ctx"], mesh.shape["head"])
    return jax.shard_map(body, mesh=mesh, in_specs=in_specs, out_specs=out_specs, check_vma=False)
```

```python
import functools

import jax
import jax.numpy as jnp
import numpy as np
from jax import lax
from jax.experimental import pallas as pl
from jax.experimental.pallas import tpu as pltpu
from jax.sharding import PartitionSpec as P

KVL = 512
NOPE = 128
ROPE = 64
VDIM = 128
LANES = KVL + ROPE

negative_fill = -1e30
softmax_scale = 0.135
rope_base = 10000.0
F32 = jnp.float32
BF16 = jnp.bfloat16
MESH = pl.DeviceIdType.MESH
strips, early_strips = 4, 1
gather_lag, reduce_lag = 4, 10


def dot_t(a, b):
    return lax.dot_general(a, b, (((1,), (1,)), ((), ())), preferred_element_type=F32)


def kernel(
    n_c, n_h, heads, rows, parts,
    qlat, lat, wq, wkv, wout, tok_h, freq_h, offset_h,
    out,
    tok, freq, offset, wq_v, wkv_v, w2, qbuf, latbuf, posbuf, qa, score, prob, attbuf,
    pa, ra, rbuf,
    lsem, qs, qr, lzs, lps, latr, xzs, xzr, xps, xpr, pzs, pzr, pps, ppr, ws, wr, ats, atr,
    gs, gr, rs, rr, os_, or_,
):
    n_z = n_c // 2
    n_lo = n_h // 2
    span = rows // parts
    piece = span // n_lo
    depth, width = wout.shape
    q_block = qbuf.shape[2]
    c = lax.axis_index("ctx")
    h = lax.axis_index("head")
    k = lax.rem(c, 2)
    z = lax.div(c, 2)
    partner = c + 1 - 2 * k
    z_of = [lax.rem(z + d, n_z) for d in range(n_z)]
    h_of = [lax.rem(h + e, n_h) for e in range(n_h)]
    shorter = jnp.minimum(z, n_z - 1 - z)
    slots = []
    for i in range(n_z):
        even = z - (i + 1) // 2 if i % 2 else z + i // 2
        single = jnp.where(2 * z < n_z, z + i - shorter, z - i + shorter)
        slots.append(jnp.where(i <= 2 * shorter, even, single))
    hi, lo = lax.div(h, n_lo), lax.rem(h, n_lo)
    lo_of = [lax.rem(lo + e, n_lo) for e in range(n_lo)]
    c_of = [2 * zz + k for zz in z_of]

    def remote(src, dst, ssem, rsem, cc, hh):
        return pltpu.make_async_remote_copy(
            src_ref=src, dst_ref=dst, send_sem=ssem, recv_sem=rsem,
            device_id=(cc, hh), device_id_type=MESH,
        )

    def slot(cc):
        return latbuf.at[cc]

    barrier = pltpu.get_barrier_semaphore()
    for d in range(1, n_z):
        pl.semaphore_signal(barrier, inc=1, device_id=(c_of[d], h), device_id_type=MESH)
    for e in range(1, n_h):
        pl.semaphore_signal(barrier, inc=1, device_id=(c, h_of[e]), device_id_type=MESH)
    pl.semaphore_signal(barrier, inc=1, device_id=(partner, h), device_id_type=MESH)

    local = [
        pltpu.make_async_copy(qlat, qbuf.at[h], lsem.at[0]),
        pltpu.make_async_copy(wq, wq_v, lsem.at[1]),
        pltpu.make_async_copy(wkv, wkv_v, lsem.at[2]),
        pltpu.make_async_copy(lat, slot(c), lsem.at[3]),
        pltpu.make_async_copy(tok_h, tok, lsem.at[4]),
        pltpu.make_async_copy(freq_h, freq, lsem.at[5]),
        pltpu.make_async_copy(offset_h, offset, lsem.at[6]),
    ]
    for copy in local:
        copy.start()
    keeps = k == hi
    across = (1 - hi) * n_lo + lo
    own_rows, other_rows = w2.at[0:depth, :], w2.at[depth:2 * depth, :]
    kept = pltpu.make_async_copy(wout, own_rows, lsem.at[7])
    pl.when(keeps)(kept.start)
    pl.semaphore_wait(barrier, n_z + n_h - 1)

    odd = lax.rem(lo, 2)
    beside = lo + 1 - 2 * odd
    peers = [(hi, beside), (1 - hi, lo), (1 - hi, beside)]
    share_rows = LANES // 36 * 5

    def part_of(a, b):
        return pl.ds(pl.multiple_of((2 * a + lax.rem(b, 2)) * share_rows, share_rows), share_rows)

    mine = part_of(hi, lo)
    both = pl.ds(4 * share_rows, LANES - 4 * share_rows)
    sends = []

    passed = []

    def send(*args):
        copy = remote(*args)
        copy.start()
        sends.append(copy)

    def start_if(ok, copy):
        pl.when(ok)(copy.start)
        passed.append((ok, copy))

    far = across
    send(lat, slot(c), lps.at[0], latr.at[c], partner, h)
    send(qlat, qbuf.at[h], qs.at[0, 0], qr.at[h], c, far)
    for e in range(1, n_lo):
        send(qlat, qbuf.at[h], qs.at[0, e], qr.at[h], c, hi * n_lo + lo_of[e])

    def strip(i):
        return pl.ds(i * (depth // strips), depth // strips)

    def cross(i):
        return remote(
            wout.at[strip(i), :], other_rows.at[strip(i), :], ws.at[i], wr.at[1 + i], c, across
        )

    def hand_on(i):
        lines = other_rows.at[strip(i), :]
        pl.when(keeps)(cross(i).wait_recv)
        start_if(keeps, remote(lines, lines, ws.at[strips + i], wr.at[1 + i], partner, h))

    for i in range(early_strips):
        start_if(jnp.logical_not(keeps), cross(i))
    away = slots[1:]
    for i, zz in enumerate(away):
        send(lat.at[mine, :], latbuf.at[c, mine, :], xzs.at[i], xzr.at[z], 2 * zz + k, h)
    for i, zz in enumerate(away):
        send(lat.at[both, :], latbuf.at[c, both, :], lzs.at[i], latr.at[c], 2 * zz + k, h)
    for i, zz in enumerate(away):
        send(tok_h, posbuf.at[k, z], pzs.at[i], pzr.at[z], 2 * zz + k, h)
    for copy in local[4:]:
        copy.wait()
    posbuf[k, z] = tok[...]

    remote(qlat, qbuf.at[far], qs.at[0, 0], qr.at[far], c, far).wait_recv()
    for e in range(1, n_lo):
        send(qbuf.at[far], qbuf.at[far], qs.at[1, e], qr.at[far], c, hi * n_lo + lo_of[e])

    for i in range(1, n_z):
        zz = slots[i]
        cc = 2 * zz + k
        remote(lat.at[mine, :], latbuf.at[cc, mine, :], xzs.at[i - 1], xzr.at[zz], cc, h).wait_recv()
        for r, (a, b) in enumerate(peers):
            block = latbuf.at[cc, mine, :]
            send(block, block, xps.at[i, r], xpr.at[zz, r], c, a * n_lo + b)

    for i in range(early_strips, strips):
        start_if(jnp.logical_not(keeps), cross(i))

    start_if(keeps, remote(wout, own_rows, ws.at[2 * strips], wr.at[0], partner, h))

    positions = jnp.transpose(jnp.broadcast_to(tok[...].astype(F32), (8, rows)))[:, 0:1]
    absolute = jnp.transpose(jnp.broadcast_to((tok[...] + offset[0]).astype(F32), (8, rows)))[:, 0:1]
    angle = absolute * freq[...]
    cosine, sine = jnp.cos(angle), jnp.sin(angle)
    cos = jnp.concatenate([cosine, cosine], axis=1)
    sin = jnp.concatenate([-sine, sine], axis=1)

    local[0].wait()
    local[1].wait()
    for e in range(1, n_lo):
        for a in (hi, 1 - hi):
            there = a * n_lo + lo_of[e]
            remote(qlat, qbuf.at[there], qs.at[0, e], qr.at[there], c, there).wait_recv()
    query = None
    for g in range(n_h):
        term = jnp.dot(qbuf[g], wq_v[g * q_block:(g + 1) * q_block, :], preferred_element_type=F32)
        query = term if query is None else query + term
    local[2].wait()
    for j in range(heads):
        base = j * (NOPE + ROPE)
        nope = query[:, base:base + NOPE].astype(BF16)
        main = dot_t(nope, wkv_v[:, j * 256:j * 256 + NOPE])
        rope = query[:, base + NOPE:base + NOPE + ROPE]
        half = ROPE // 2
        swapped = jnp.concatenate([rope[:, half:], rope[:, :half]], axis=1)
        rotated = rope * cos + swapped * sin
        for p in range(parts):
            lines = slice((p * heads + j) * span, (p * heads + j + 1) * span)
            qa[lines, 0:KVL] = main[p * span:(p + 1) * span].astype(BF16)
            qa[lines, KVL:LANES] = rotated[p * span:(p + 1) * span].astype(BF16)

    for i in range(1, n_z):
        zz = slots[i]
        cc = 2 * zz + k
        remote(lat.at[both, :], latbuf.at[cc, both, :], lzs.at[i - 1], latr.at[cc], cc, h).wait_recv()
        for r, (a, b) in enumerate(peers):
            block = latbuf.at[cc, part_of(a, b), :]
            remote(block, block, xps.at[i, r], xpr.at[zz, r], c, a * n_lo + b).wait_recv()
        send(slot(cc), slot(cc), lps.at[i], latr.at[cc], partner, h)
    for i in range(1, n_z):
        zz = slots[i]
        remote(tok, posbuf.at[k, zz], pzs.at[i - 1], pzr.at[zz], 2 * zz + k, h).wait_recv()
    send(posbuf.at[k], posbuf.at[k], pps, ppr, partner, h)
    local[3].wait()
    for i in range(n_z):
        cc = 2 * slots[i] + 1 - k
        remote(lat, slot(cc), lps.at[i], latr.at[cc], partner, h).wait_recv()
    remote(posbuf.at[1 - k], posbuf.at[1 - k], pps, ppr, partner, h).wait_recv()
    for i in range(2):
        hand_on(i)
    key_pos = jnp.concatenate([posbuf[cc % 2, cc // 2] for cc in range(n_c)], axis=1).astype(F32)
    latents = jnp.concatenate([latbuf[cc] for cc in range(n_c)], axis=1)
    def pass_on(zz, p, row, to):
        lines = attbuf.at[zz, p * span:(p + 1) * span, 0:depth]
        return remote(lines, lines, ats.at[row, p], atr.at[zz, p], 2 * to + k, h)

    def share(d):
        zz, p = slots[d // parts], d % parts
        lines = attbuf.at[zz, p * span:(p + 1) * span, :]
        return remote(
            lines.at[:, 0:depth], lines.at[:, depth:2 * depth], gs.at[d], gr.at[d], c, across
        )

    score[...] = jnp.dot(qa[...], latents, preferred_element_type=F32)
    for p in range(parts):
        visible = key_pos <= positions[p * span:(p + 1) * span]
        sums = []
        for j in range(heads):
            lines = slice((p * heads + j) * span, (p * heads + j + 1) * span)
            s = jnp.where(visible, score[lines, :] * softmax_scale, negative_fill)
            largest = jnp.max(s, axis=-1, keepdims=True)
            weights = jnp.exp(s - largest)
            sums.append(jnp.sum(weights, axis=-1, keepdims=True))
            prob[lines, :] = weights.astype(BF16)
        lines = slice(p * heads * span, (p + 1) * heads * span)
        summed = dot_t(prob[lines, :], latents[0:KVL, :])
        for j in range(heads):
            normed = (summed[j * span:(j + 1) * span, :] / sums[j]).astype(BF16)
            value = jnp.dot(normed, wkv_v[:, j * 256 + NOPE:(j + 1) * 256], preferred_element_type=F32)
            attbuf[z, p * span:(p + 1) * span, j * VDIM:(j + 1) * VDIM] = value.astype(BF16)
        start_if(z + 1 < n_z, pass_on(z, p, 0, z + 1))
        start_if(z > 0, pass_on(z, p, n_z, z - 1))
        share(p).start()

    def arrive(d):
        if d >= parts:
            zz, p = slots[d // parts], d % parts
            onward = jnp.where(zz < z, z + 1, z - 1)
            pass_on(zz, p, d // parts, z).wait_recv()
            start_if((onward >= 0) & (onward < n_z), pass_on(zz, p, d // parts, onward))
            share(d).start()

    def project(d):
        share(d).wait_recv()
        lines = attbuf[slots[d // parts], d % parts * span:(d % parts + 1) * span, :]
        part = jnp.dot(lines, w2[...], preferred_element_type=F32).astype(BF16)
        for i in range(n_lo):
            pa[d, i] = part[i * piece:(i + 1) * piece, :]
        for e in range(1, n_lo):
            send(pa.at[d, lo_of[e]], ra.at[d, lo], rs.at[d, e], rr.at[d, lo], c, hi * n_lo + lo_of[e])

    def place(side, p, line):
        if width % 128:
            return out.at[side, p, line]
        return out.at[p, line, :, pl.ds(pl.multiple_of(side * width, 128), width)]

    def deliver(d):
        return remote(
            rbuf.at[d], place(hi, d % parts, lo), os_.at[d], or_.at[d % parts, h],
            2 * slots[d // parts] + k, z,
        )

    def reduce(d):
        total = pa[d, lo].astype(F32)
        for e in range(1, n_lo):
            ll = lo_of[e]
            remote(pa.at[d, ll], ra.at[d, ll], rs.at[d, e], rr.at[d, ll], c, hi * n_lo + ll).wait_recv()
            total = total + ra[d, ll].astype(F32)
        rbuf[d] = total.astype(BF16)
        if d < parts:
            pl.when(z != h)(deliver(d).start)

            @pl.when(z == h)
            def _():
                place(hi, d % parts, lo)[...] = rbuf[d]
        else:
            deliver(d).start()

    def weights():
        pl.when(keeps)(kept.wait)
        for i in range(2, strips):
            hand_on(i)

        @pl.when(jnp.logical_not(keeps))
        def _():
            remote(wout, own_rows, ws.at[2 * strips], wr.at[0], partner, h).wait_recv()
            for i in range(strips):
                lines = other_rows.at[strip(i), :]
                remote(lines, lines, ws.at[strips + i], wr.at[1 + i], partner, h).wait_recv()

    chunks = n_z * parts
    for d in range(chunks + reduce_lag):
        if d < chunks:
            arrive(d)
        if d == gather_lag:
            weights()
        if 0 <= d - gather_lag < chunks:
            project(d - gather_lag)
        if 0 <= d - reduce_lag < chunks:
            reduce(d - reduce_lag)
    for hh in range(n_h):
        @pl.when((z != h) | (h != hh))
        def _():
            for p in range(parts):
                remote(
                    rbuf.at[0], place(hh // n_lo, p, hh % n_lo), os_.at[0], or_.at[p, hh], c, h
                ).wait_recv()
    for d in range(chunks):
        share(d).wait_send()
        if d >= parts:
            deliver(d).wait_send()
        else:
            pl.when(z != h)(deliver(d).wait_send)
    for ok, copy in passed:
        pl.when(ok)(copy.wait_send)
    for copy in sends:
        copy.wait_send()


def shards(n_c, n_h, q_latent, latent_cache, w_q_up, w_kv_up, w_out, token_pos, start_offset):
    rows, q_block = q_latent.shape
    heads = w_q_up.shape[1] // (NOPE + ROPE)
    n_z, n_lo = n_c // 2, n_h // 2
    assert n_z == n_h
    keys = n_c * rows
    width = w_out.shape[1]
    parts = 2 if rows // n_lo >= 32 else 1
    piece = rows // n_lo // parts
    chunks = n_z * parts
    split = 1 if width % 128 else 0
    freqs = rope_base ** (-np.arange(ROPE // 2) * 2.0 / ROPE)
    dma = pltpu.SemaphoreType.DMA
    anywhere = pl.BlockSpec(memory_space=pltpu.HBM)
    vmem = pl.BlockSpec(memory_space=pltpu.VMEM)
    result = pl.pallas_call(
        functools.partial(kernel, n_c, n_h, heads, rows, parts),
        out_shape=pltpu.VMEM((2,) * split + (parts, n_lo, piece, (2 - split) * width), BF16),
        in_specs=[anywhere] * 8,
        out_specs=vmem,
        scratch_shapes=[
            pltpu.VMEM((1, rows), jnp.int32),
            pltpu.VMEM((1, ROPE // 2), F32),
            pltpu.SMEM((1,), jnp.int32),
            pltpu.VMEM(w_q_up.shape, BF16),
            pltpu.VMEM(w_kv_up.shape, BF16),
            pltpu.VMEM((2 * w_out.shape[0], width), BF16),
            pltpu.VMEM((n_h, rows, q_block), BF16),
            pltpu.VMEM((n_c, LANES, rows), BF16),
            pltpu.VMEM((2, n_z, 1, rows), jnp.int32),
            pltpu.VMEM((heads * rows, LANES), BF16),
            pltpu.VMEM((heads * rows, keys), F32),
            pltpu.VMEM((heads * rows, keys), BF16),
            pltpu.VMEM((n_z, rows, 2 * heads * VDIM), BF16),
            pltpu.VMEM((chunks, n_lo, piece, width), BF16),
            pltpu.VMEM((chunks, n_lo, piece, width), BF16),
            pltpu.VMEM((chunks, piece, width), BF16),
            dma((8,)),
            dma((2, n_lo)), dma((n_h,)),
            dma((n_z,)), dma((n_z,)), dma((n_c,)),
            dma((n_z,)), dma((n_z,)), dma((n_z, 3)), dma((n_z, 3)),
            dma((n_z,)), dma((n_z,)), dma, dma,
            dma((2 * strips + 1,)), dma((1 + strips,)),
            dma((n_z + 1, parts)), dma((n_z, parts)),
            dma((chunks,)), dma((chunks,)),
            dma((chunks, n_lo)), dma((chunks, n_lo)),
            dma((chunks,)), dma((parts, n_h)),
        ],
        compiler_params=pltpu.CompilerParams(
            collective_id=0, has_side_effects=True, vmem_limit_bytes=67043328 - (768 << 10)
        ),
        name="mla",
    )(q_latent, latent_cache.T, w_q_up, w_kv_up, w_out, token_pos[None, :], freqs.astype(np.float32)[None, :], start_offset)
    if not split:
        return result.reshape(rows, 2 * width)
    result = result.reshape(2, rows, width)
    return jnp.concatenate([result[0], result[1]], axis=1)


def solution(mesh):
    in_specs = (
        P("ctx", "head"),
        P("ctx", None),
        P(None, "head"),
        P(None, "head"),
        P("head", "ctx"),
        P("ctx"),
        P(),
    )
    out_specs = P("ctx", "head")
    body = functools.partial(shards, mesh.shape["ctx"], mesh.shape["head"])
    return jax.shard_map(body, mesh=mesh, in_specs=in_specs, out_specs=out_specs, check_vma=False)
```
